256 devices in a mesh: chan: 4 (over x), vox: 64 (over y, z, core).
Axes of the slice: x: 4, y: 4, z: 8, core: 2. Of those that a mesh axis runs over, the one named last changes fastest.
Arguments:
- echo_data: bfloat16 [1024, 64, 6400], P('chan', 'vox'), may hold values from -60 to 60
- delays: int32 [1024, 64], P('chan', 'vox'), may hold values from 0 to 64, as said below
- aperture: int32 [128, 64], replicated, may hold values from 0 to 1, as said below
- offset: float32 [128, 64], P(None, 'vox'), may hold values from 0.5 to 3.2
- depth_slope: float32 [128, 64], P(None, 'vox'), may hold values from 0.3 to 0.4
- lateral_tilt: float32 [128, 64], P(None, 'vox'), may hold values from 0.075 to 0.125
- prior_basis: float32 [100, 30], replicated, may hold values from -6 to 6
Outputs:
- power: float32 [64, 16384], P('vox', 'chan')
The draws below stay inside these ranges and needn't reach their ends.
Inputs may be any that keep to these rules, and one draw needn't show every extreme that they name: `delays`: every slab has a channel whose delay is 64. `aperture`: for each slab, the active blocks among the 32 blocks of one channel group (blocks g * 32 onward) form one cyclic run of at least 4 and at most 16 blocks; each channel group has exactly 16 active blocks in some slab.
All inputs are finite; a program needn't handle non-finite values.
Results may differ from the reference program's by a relative error of at most 0.0075.
Values may be sent and summed in bfloat16 or wider, within the bound.
A program may use at most 128 MiB of HBM per device.

```python
import math
import jax
import jax.numpy as jnp
from jax import lax

CHANNELS = 1024
FRAMES = 100
BASIS_RANK = 30
BLOCK_CH = 8
WINDOW = 64
DEPTH_VOX = 64
ACTIVE_MOST = 16
SLABS = 64
SLAB_VOX = 16384
BLOCKS = 128
BLOCKS_DEV = 32
N_CHAN = 4


def draw_echo_data(key, part):
    keys = jax.random.split(jax.random.fold_in(key, 101), 5)
    samples = WINDOW * SLABS
    frame_modes = jax.random.normal(keys[0], (FRAMES, BASIS_RANK), jnp.float32)
    channel_mix = jax.random.normal(keys[1], (CHANNELS, BASIS_RANK), jnp.float32)
    sample_mix = jax.random.normal(keys[2], (BASIS_RANK, samples), jnp.float32)
    amplitude = jnp.exp(jax.random.uniform(keys[3], (BASIS_RANK, SLABS), jnp.float32, math.log(0.3), math.log(3.0)))
    noise = jax.random.normal(keys[4], (CHANNELS, FRAMES, samples), jnp.float32)
    sample_mix = sample_mix * jnp.repeat(amplitude, WINDOW, axis=1) / math.sqrt(BASIS_RANK)
    clutter = jnp.einsum('fr,cr,rs->cfs', frame_modes, channel_mix, sample_mix)
    slab_index = (jnp.arange(samples) // WINDOW).astype(jnp.float32)
    growth = jnp.exp(math.log(3.0) * slab_index / max(SLABS - 1, 1))
    values = jnp.clip((noise + clutter) * growth[None, None, :], -60.0, 60.0)
    values = jnp.transpose(values.reshape(CHANNELS, FRAMES, SLABS, WINDOW), (0, 2, 1, 3))
    return values.reshape(CHANNELS, SLABS, FRAMES * WINDOW).astype(jnp.bfloat16)


def draw_delays(key, part):
    keys = jax.random.split(jax.random.fold_in(key, 202), 2)
    values = jax.random.randint(keys[0], (CHANNELS, SLABS), 0, WINDOW + 1, jnp.int32)
    chosen = jax.random.randint(keys[1], (SLABS,), 0, CHANNELS, jnp.int32)
    channel_ids = jnp.arange(CHANNELS, dtype=jnp.int32)
    return jnp.where(channel_ids[:, None] == chosen[None, :], WINDOW, values).astype(jnp.int32)


def draw_aperture(key, part):
    keys = jax.random.split(jax.random.fold_in(key, 303), 3)
    groups = BLOCKS // BLOCKS_DEV
    least = max(1, ACTIVE_MOST // 4)
    counts = jax.random.randint(keys[0], (groups, SLABS), least, ACTIVE_MOST + 1, jnp.int32)
    fullest = jax.random.randint(keys[1], (groups,), 0, SLABS, jnp.int32)
    slab_ids = jnp.arange(SLABS, dtype=jnp.int32)
    counts = jnp.where(slab_ids[None, :] == fullest[:, None], ACTIVE_MOST, counts)
    starts = jax.random.randint(keys[2], (groups, SLABS), 0, BLOCKS_DEV, jnp.int32)
    block_ids = jnp.arange(BLOCKS_DEV, dtype=jnp.int32)
    relative = (block_ids[None, None, :] - starts[:, :, None]) % BLOCKS_DEV
    active = (relative < counts[:, :, None]).astype(jnp.int32)
    return jnp.transpose(active, (0, 2, 1)).reshape(BLOCKS, SLABS).astype(jnp.int32)


def block_scale(key, shape, cuts, low, top_value):
    gain = 1.0
    for dim, parts in cuts:
        heights = jax.random.uniform(jax.random.fold_in(jax.random.fold_in(key, 6), dim), (parts,), jnp.float32, low / len(cuts), top_value / len(cuts))
        gain = gain * jnp.repeat(jnp.exp(heights), shape[dim] // parts).reshape((-1,) + (1,) * (len(shape) - 1 - dim))
    return gain


def scatter_about(own_key, extent, scale, bound, held_as=jnp.bfloat16):
    array = scale * jax.random.normal(own_key, extent, jnp.float32)
    return jnp.clip(array, min=-bound, max=bound).astype(held_as)


def setup_inputs(seed: int = 0) -> dict:
    splits = jax.random.split(jax.random.key(seed), 8)
    echo_data = draw_echo_data(jax.random.fold_in(splits[7], 71), 0)
    delays = draw_delays(jax.random.fold_in(splits[7], 71), 0)
    aperture = draw_aperture(jax.random.fold_in(splits[7], 71), 0)
    offset = jnp.clip(0.5 + 2.7 * jax.random.uniform(splits[3], (BLOCKS, SLABS), jnp.float32) ** block_scale(splits[3], (BLOCKS, SLABS), ((1, 64),), -0.2, 0.2), 0.5, 3.2)
    depth_slope = jnp.clip(0.3 + 0.099999994 * jax.random.uniform(splits[4], (BLOCKS, SLABS), jnp.float32) ** block_scale(splits[4], (BLOCKS, SLABS), ((1, 64),), -0.2, 0.2), 0.3, 0.4)
    lateral_tilt = jnp.clip(0.075 + 0.049999997 * jax.random.uniform(splits[5], (BLOCKS, SLABS), jnp.float32) ** block_scale(splits[5], (BLOCKS, SLABS), ((1, 64),), -0.2, 0.2), 0.075, 0.125)
    prior_basis = scatter_about(splits[6], (FRAMES, BASIS_RANK), 1.0, 6.0, jnp.float32)
    return dict(echo_data=echo_data, delays=delays, aperture=aperture, offset=offset, depth_slope=depth_slope, lateral_tilt=lateral_tilt, prior_basis=prior_basis)


def interp_table(offsets, slopes, tilts):
    voxel = jnp.arange(SLAB_VOX)
    lateral = (voxel // DEPTH_VOX).astype(jnp.float32)
    depth = (voxel % DEPTH_VOX).astype(jnp.float32)
    position = offsets[:, None] + slopes[:, None] * depth[None, :] + tilts[:, None] * lateral[None, :]
    sample_rows = jnp.arange(WINDOW).astype(jnp.float32)
    weights = jnp.maximum(0.0, 1.0 - jnp.abs(sample_rows[None, :, None] - position[:, None, :]))
    return (weights / math.sqrt(CHANNELS)).astype(jnp.bfloat16)

def take_window(row, start):
    return lax.dynamic_slice(row, (jnp.zeros((), jnp.int32), start.astype(jnp.int32)), (FRAMES, WINDOW))

def refine_basis(gram_matrix, prior_basis):
    basis = prior_basis
    for sweep in range(2):
        product = jnp.dot(gram_matrix, basis, precision=lax.Precision.HIGHEST)
        normal_matrix = jnp.dot(product.T, product, precision=lax.Precision.HIGHEST)
        factor = jnp.linalg.cholesky(normal_matrix)
        basis = jax.scipy.linalg.solve_triangular(factor, product.T, lower=True).T
    return basis

def reference(echo_data, delays, aperture, offset, depth_slope, lateral_tilt, prior_basis):

    def beam_slab(slab):
        own_part = lax.dynamic_index_in_dim(echo_data, slab, 1, keepdims=False).reshape(CHANNELS, FRAMES, WINDOW)
        next_slab = jnp.minimum(slab + 1, SLABS - 1)
        next_part = lax.dynamic_index_in_dim(echo_data, next_slab, 1, keepdims=False).reshape(CHANNELS, FRAMES, WINDOW)
        next_part = jnp.where(slab + 1 < SLABS, next_part, jnp.zeros_like(next_part))
        extended = jnp.concatenate([own_part, next_part], axis=2)
        slab_delays = lax.dynamic_index_in_dim(delays, slab, 1, keepdims=False)
        windows = jax.vmap(take_window)(extended, slab_delays)
        gates = lax.dynamic_index_in_dim(aperture, slab, 1, keepdims=False).astype(jnp.float32)
        summed = lax.optimization_barrier(jnp.sum(windows.astype(jnp.float32).reshape(BLOCKS, BLOCK_CH, FRAMES, WINDOW), axis=1))
        summed = (summed * gates[:, None, None]).astype(jnp.bfloat16)
        table = interp_table(lax.dynamic_index_in_dim(offset, slab, 1, keepdims=False), lax.dynamic_index_in_dim(depth_slope, slab, 1, keepdims=False), lax.dynamic_index_in_dim(lateral_tilt, slab, 1, keepdims=False))
        partial_value = jnp.einsum('gbfk,gbkv->gfv', summed.reshape(N_CHAN, BLOCKS_DEV, FRAMES, WINDOW).astype(jnp.float32), table.reshape(N_CHAN, BLOCKS_DEV, WINDOW, SLAB_VOX).astype(jnp.float32), precision=lax.Precision.HIGHEST)
        rounded = lax.optimization_barrier(partial_value.astype(jnp.bfloat16))
        return lax.optimization_barrier(jnp.sum(rounded.astype(jnp.float32), axis=0))
    beam = lax.map(beam_slab, jnp.arange(SLABS))
    gram_matrix = jnp.einsum('sfv,sgv->fg', beam, beam, precision=lax.Precision.HIGHEST)
    basis = refine_basis(gram_matrix, prior_basis)
    coefficients = jnp.einsum('fr,sfv->srv', basis, beam, precision=lax.Precision.HIGHEST)
    clean = beam - jnp.einsum('fr,srv->sfv', basis, coefficients, precision=lax.Precision.HIGHEST)
    return lax.optimization_barrier(jnp.sum(clean * clean, axis=1)) / FRAMES
```

```python
import functools

import jax
import jax.numpy as jnp
from jax import lax
from jax.experimental import pallas as pl
from jax.experimental.pallas import tpu as pltpu
from jax.sharding import PartitionSpec as P

MESH = pl.DeviceIdType.MESH
FRAMES = 100
RANK = 30
PAIRS = 50
ROWS = 64
RUN = 16
GROUP = 32
SLABS = 64
BAND = 32
VMEM = pltpu.VMEM
F32 = jnp.float32
BF16 = jnp.bfloat16


def iota(shape, dim):
    return lax.broadcasted_iota(jnp.int32, shape, dim)


def active_run(row, group):
    lane = iota(row.shape, 1)
    before = jnp.where(lane % GROUP == 0, pltpu.roll(row, 97, 1), pltpu.roll(row, 1, 1))
    mine = (lane // GROUP == group).astype(jnp.int32)
    first = (row * (1 - before) * mine * (lane % GROUP)).astype(F32)
    start = jnp.sum(first).astype(jnp.int32)
    count = jnp.sum((row * mine).astype(F32)).astype(jnp.int32)
    return start, count


def window_kernel(own, aperture_ref, delay_ref, echo_ref, out_ref, moved_ref, rows_ref):
    group = lax.axis_index("chan")
    slab = lax.axis_index("vox")
    if not own:
        slab = lax.rem(slab + SLABS - 1, SLABS)
    row = aperture_ref[pl.ds(slab, 1), :]
    start, count = active_run(row, group)
    lane = iota((8, 128), 1)
    sub = iota((8, 128), 0)
    sample = lane & 63
    low = jnp.broadcast_to(delay_ref[0:1, 0:128], (8, 128))
    high = jnp.broadcast_to(delay_ref[0:1, 128:256], (8, 128))

    def pair(i, carry):
        blocks, picks, keeps = [], [], []
        for q in range(2):
            block = lax.rem(start + 2 * i + q, GROUP)
            table = jnp.where(block < 16, low, high)
            delay = jnp.take_along_axis(table, (block & 15) * 8 + sub, axis=1)
            if own:
                picks.append((lane + delay) & 127)
                keeps.append(sample + delay < 64)
            else:
                picks.append((lane + delay + 64) & 127)
                keeps.append(sample + delay >= 64)
            blocks.append(block)
        for t in range(PAIRS):
            parts = []
            for q in range(2):
                values = echo_ref[blocks[q], :, t * 128 : (t + 1) * 128].astype(F32)
                values = jnp.take_along_axis(values, picks[q], axis=1)
                parts.append(jnp.where(keeps[q], values, 0.0))
            moved_ref[pl.ds(i * 16, 16), t * 128 : (t + 1) * 128] = jnp.concatenate(
                parts, axis=0
            ).astype(BF16)
        return carry

    lax.fori_loop(0, RUN // 2, pair, 0)
    rows_ref[...] = jnp.zeros_like(rows_ref)
    block_of = iota((RUN, 128), 0)
    gather = (iota((RUN, 128), 1) // 8 == block_of) & (block_of < count)
    gather = jnp.where(gather, 1.0 / 32, 0.0).astype(BF16)
    for c in range(PAIRS // 2):
        sums = jnp.dot(
            gather, moved_ref[:, c * 256 : (c + 1) * 256], preferred_element_type=F32
        )
        for q in range(2):
            for h in range(2):
                rows_ref[pl.ds(h * 8 * ROWS + 2 * c + q, 8, stride=ROWS), :] = sums[
                    h * 8 : h * 8 + 8, q * 128 : (q + 1) * 128
                ]
    out_ref[...] = rows_ref[...].astype(out_ref.dtype)


def window_sums(own, aperture, delay, echo):
    return pl.pallas_call(
        functools.partial(window_kernel, own),
        out_shape=jax.ShapeDtypeStruct((RUN * ROWS, 128), F32 if own else BF16),
        in_specs=[pl.BlockSpec(memory_space=VMEM)] * 3,
        out_specs=pl.BlockSpec(memory_space=VMEM),
        scratch_shapes=[VMEM((128, 128 * PAIRS), BF16), VMEM((RUN * ROWS, 128), F32)],
        name="window_own" if own else "window_prev",
        cost_estimate=pl.CostEstimate(flops=10**8, bytes_accessed=4 * 10**6, transcendentals=0),
    )(aperture, delay, echo)


def share_kernel(own_ref, prev_ref, out_ref, next_ref, all_ref, send, recv, peer_send, peer_recv):
    group = lax.axis_index("chan")
    slab = lax.axis_index("vox")
    before = lax.rem(slab + SLABS - 1, SLABS)
    after = lax.rem(slab + 1, SLABS)
    peers = [lax.rem(group + d, 4) for d in range(1, 4)]
    barrier = pltpu.get_barrier_semaphore()
    for place in [(group, before), (group, after)] + [(p, slab) for p in peers]:
        pl.semaphore_signal(barrier, inc=1, device_id=place, device_id_type=MESH)
    pl.semaphore_wait(barrier, 5)
    copy = pltpu.make_async_remote_copy(
        src_ref=prev_ref,
        dst_ref=next_ref,
        send_sem=send,
        recv_sem=recv,
        device_id=(group, before),
        device_id_type=MESH,
    )
    copy.start()
    copy.wait()
    live = jnp.where(slab < SLABS - 1, 1.0, 0.0)
    size = RUN * ROWS
    all_ref[pl.ds(pl.multiple_of(group * size, size), size), :] = (
        own_ref[...] + next_ref[...].astype(F32) * live
    ).astype(BF16)
    here = all_ref.at[pl.ds(pl.multiple_of(group * size, size), size), :]
    copies = []
    for d in range(3):
        copies.append(
            pltpu.make_async_remote_copy(
                src_ref=here,
                dst_ref=here,
                send_sem=peer_send.at[d],
                recv_sem=peer_recv.at[d],
                device_id=(peers[d], slab),
                device_id_type=MESH,
            )
        )
    for c in copies:
        c.start()
    for c in copies:
        c.wait()
    out_ref[...] = all_ref[...]


def share(own, prev):
    return pl.pallas_call(
        share_kernel,
        out_shape=jax.ShapeDtypeStruct((4 * RUN * ROWS, 128), BF16),
        in_specs=[pl.BlockSpec(memory_space=VMEM)] * 2,
        out_specs=pl.BlockSpec(memory_space=VMEM),
        scratch_shapes=[
            VMEM((RUN * ROWS, 128), BF16),
            VMEM((4 * RUN * ROWS, 128), BF16),
            pltpu.SemaphoreType.DMA,
            pltpu.SemaphoreType.DMA,
            pltpu.SemaphoreType.DMA((3,)),
            pltpu.SemaphoreType.DMA((3,)),
        ],
        compiler_params=pltpu.CompilerParams(collective_id=0, has_side_effects=True),
        name="share",
    )(own, prev)


def project_kernel(
    aperture_ref, offset_ref, slope_ref, tilt_ref, all_ref, beam_ref, gram_ref, lhs_ref, geo_ref
):
    group = lax.axis_index("chan")
    slab = lax.axis_index("vox")
    row = aperture_ref[pl.ds(slab, 1), :]
    lane8 = iota((8, 128), 1)
    slot = lane8 // BAND
    for g in range(4):
        start, _ = active_run(row, g)

        def quad(q, carry):
            sums = [[[None] * 8 for par in range(2)] for h in range(2)]
            for k in range(4):
                j = q * 4 + k
                block = g * GROUP + lax.rem(start + j, GROUP)
                offset = offset_ref[0, block]
                tilt = tilt_ref[0, block]
                place = g * RUN + j
                geo_ref[2, place] = slope_ref[0, block]
                geo_ref[3, place] = tilt
                picks = []
                for h in range(2):
                    origin = offset + tilt * (64 * group + 32 * h).astype(F32)
                    first = origin.astype(jnp.int32)
                    geo_ref[h, place] = origin - first.astype(F32)
                    picks.append(first + (lane8 & (BAND - 1)))
                base = pl.multiple_of(place * ROWS, ROWS)
                for r in range(4):
                    part = all_ref[pl.ds(base + r * 16, 16), :].astype(F32)
                    for half in range(2):
                        values = part[half * 8 : half * 8 + 8]
                        for h in range(2):
                            for par in range(2):
                                got = jnp.take_along_axis(
                                    values, (picks[h] + 64 * par) & 127, axis=1
                                )
                                old = sums[h][par][2 * r + half]
                                sums[h][par][2 * r + half] = (
                                    got if old is None else jnp.where(slot == k, got, old)
                                )
            for h in range(2):
                for par in range(2):
                    lhs_ref[
                        h,
                        par * ROWS : (par + 1) * ROWS,
                        pl.ds(pl.multiple_of((g * 4 + q) * 128, 128), 128),
                    ] = jnp.concatenate(sums[h][par], axis=0).astype(BF16)
            return carry

        lax.fori_loop(0, 4, quad, 0)

    gram_ref[...] = jnp.zeros_like(gram_ref)
    depth = (lane8 & 63).astype(F32)
    band = iota((8, 128), 0).astype(F32)

    for h in range(2):

        def tile(n, carry):
            total = jnp.zeros((128, 256), F32)
            for c in range(8):
                rows = []
                for b in range(8):
                    place = c * 8 + b
                    origin = geo_ref[h, place]
                    slope = geo_ref[2, place]
                    tilt = geo_ref[3, place]
                    columns = []
                    for i in range(2):
                        lateral = ((lane8 >> 6) + 2 * i + 4 * n).astype(F32)
                        position = origin + slope * depth + tilt * lateral
                        parts = [
                            jnp.maximum(0.0, 1.0 - jnp.abs(band + (8.0 * k) - position))
                            for k in range(4)
                        ]
                        columns.append(jnp.concatenate(parts, axis=0).astype(BF16))
                    rows.append(jnp.concatenate(columns, axis=1))
                table = jnp.concatenate(rows, axis=0)
                total = total + jnp.dot(
                    lhs_ref[h, :, c * 256 : (c + 1) * 256], table, preferred_element_type=F32
                )
            high = total.astype(BF16)
            low = (total - high.astype(F32)).astype(BF16)
            both = jnp.concatenate([high, low], axis=0)
            beam_ref[:, pl.ds(pl.multiple_of((h * 8 + n) * 256, 256), 256)] = both
            gram_ref[...] += lax.dot_general(
                both, both, (((1,), (1,)), ((), ())), preferred_element_type=F32
            )
            return carry

        lax.fori_loop(0, 8, tile, 0)


def project(aperture, offset, slope, tilt, everything):
    smem = pl.BlockSpec(memory_space=pltpu.SMEM)
    vmem = pl.BlockSpec(memory_space=VMEM)
    beam, gram = pl.pallas_call(
        project_kernel,
        out_shape=(
            jax.ShapeDtypeStruct((256, 4096), BF16),
            jax.ShapeDtypeStruct((256, 256), F32),
        ),
        in_specs=[vmem, smem, smem, smem, vmem],
        out_specs=(vmem, vmem),
        scratch_shapes=[VMEM((2, 128, 64 * BAND), BF16), pltpu.SMEM((4, 64), F32)],
        name="project",
    )(aperture, offset, slope, tilt, everything)
    return beam, gram


def sweep(gram, rows):
    product = jnp.dot(rows, gram, precision=lax.Precision.HIGHEST, preferred_element_type=F32)
    normal = lax.dot_general(
        product,
        product,
        (((1,), (1,)), ((), ())),
        precision=lax.Precision.HIGHEST,
        preferred_element_type=F32,
    )
    normal = jnp.concatenate([normal, jnp.zeros((32, 96), F32)], axis=1)
    sub = iota((32, 128), 0)
    scale = jnp.zeros((32, 128), F32)
    for j in range(RANK):
        column = jnp.take_along_axis(normal, jnp.full((32, 128), j, jnp.int32), axis=1)
        pivot = jnp.broadcast_to(column[j : j + 1], (32, 128))
        scale = jnp.where(sub == j, lax.rsqrt(pivot), scale)
        factor = jnp.where(sub > j, column / pivot, 0.0)
        normal = normal - factor * normal[j : j + 1]
        product = product - factor * product[j : j + 1]
    return product * scale


def filter_kernel(gram_ref, prior_ref, beam_ref, out_ref):
    gram = gram_ref[...]
    lane = iota((32, 128), 1)
    pick = jnp.minimum(2 * (lane & 63) + (lane >> 6), 127)
    rows = jnp.take_along_axis(prior_ref[...], pick, axis=1)
    rows = jnp.where((lane & 63) < PAIRS, rows, 0.0)
    rows = sweep(gram, rows)
    rows = sweep(gram, rows)
    overlap = lax.dot_general(
        rows,
        rows,
        (((0,), (0,)), ((), ())),
        precision=lax.Precision.HIGHEST,
        preferred_element_type=F32,
    )
    keep = jnp.where(iota((128, 128), 0) == iota((128, 128), 1), 1.0, 0.0) - overlap
    high = keep.astype(BF16)
    low = (keep - high.astype(F32)).astype(BF16)
    twice = jnp.concatenate([high, high], axis=1)
    for c in range(16):
        beam = beam_ref[:, c * 256 : (c + 1) * 256]
        clean = jnp.dot(twice, beam, preferred_element_type=F32)
        clean = clean + jnp.dot(low, beam[0:128], preferred_element_type=F32)
        out_ref[:, c * 256 : (c + 1) * 256] = jnp.sum(
            clean * clean, axis=0, keepdims=True
        ) * (1.0 / FRAMES)


def combine_kernel(wide_ref, out_ref, mine_ref, got_ref, sum_ref, all_ref, send, recv):
    group = lax.axis_index("chan")
    slab = lax.axis_index("vox")
    core = lax.rem(slab, 2)
    chip = slab // 2
    y, z = chip // 8, lax.rem(chip, 8)
    me = group * 2 + core
    around = []
    for d in range(1, 8):
        peer = lax.rem(me + d, 8)
        around.append((peer, (peer // 2, slab - core + lax.rem(peer, 2))))
    along_y = [(group, (lax.rem(y + d, 4) * 8 + z) * 2 + core) for d in range(1, 4)]
    along_z = [(group, (y * 8 + lax.rem(z + d, 8)) * 2 + core) for d in range(1, 8)]
    barrier = pltpu.get_barrier_semaphore()
    for place in [a[1] for a in around] + along_y + along_z:
        pl.semaphore_signal(barrier, inc=1, device_id=place, device_id_type=MESH)
    mine_ref[...] = (
        wide_ref[0:128, 0:128]
        + wide_ref[128:256, 0:128]
        + wide_ref[0:128, 128:256]
        + wide_ref[128:256, 128:256]
    )
    pl.semaphore_wait(barrier, 17)

    def copy(src, dst, place, k):
        return pltpu.make_async_remote_copy(
            src_ref=src,
            dst_ref=dst,
            send_sem=send.at[k],
            recv_sem=recv.at[k],
            device_id=place,
            device_id_type=MESH,
        )

    def rows(k):
        return pl.ds(pl.multiple_of(k * 16, 16), 16)

    copies = [
        copy(mine_ref.at[rows(peer)], got_ref.at[k], place, k)
        for k, (peer, place) in enumerate(around)
    ]
    for c in copies:
        c.start()
    for c in copies:
        c.wait()
    total = mine_ref[rows(me), :]
    for k in range(7):
        total = total + got_ref[k]
    sum_ref[0] = total
    copies = [copy(sum_ref.at[0], got_ref.at[7 + k], p, 7 + k) for k, p in enumerate(along_y)]
    for c in copies:
        c.start()
    for c in copies:
        c.wait()
    for k in range(3):
        total = total + got_ref[7 + k]
    sum_ref[1] = total
    copies = [copy(sum_ref.at[1], got_ref.at[10 + k], p, 10 + k) for k, p in enumerate(along_z)]
    for c in copies:
        c.start()
    for c in copies:
        c.wait()
    for k in range(7):
        total = total + got_ref[10 + k]
    here = all_ref.at[rows(me), :]
    all_ref[rows(me), :] = total
    copies = [copy(here, here, place, 17 + k) for k, (_, place) in enumerate(around)]
    for c in copies:
        c.start()
    for c in copies:
        c.wait()
    out_ref[...] = all_ref[...]


def combine(gram):
    return pl.pallas_call(
        combine_kernel,
        out_shape=jax.ShapeDtypeStruct((128, 128), F32),
        in_specs=[pl.BlockSpec(memory_space=VMEM)],
        out_specs=pl.BlockSpec(memory_space=VMEM),
        scratch_shapes=[
            VMEM((128, 128), F32),
            VMEM((17, 16, 128), F32),
            VMEM((2, 16, 128), F32),
            VMEM((128, 128), F32),
            pltpu.SemaphoreType.DMA((24,)),
            pltpu.SemaphoreType.DMA((24,)),
        ],
        compiler_params=pltpu.CompilerParams(collective_id=1, has_side_effects=True),
        name="combine",
    )(gram)


def body(echo_data, delays, aperture, offset, depth_slope, lateral_tilt, prior_basis):
    echo = echo_data.reshape(32, 8, 6400)
    delay = delays.reshape(1, 256)
    own_aperture = aperture.T
    prev_delay = lax.ppermute(delay, "vox", [(i, (i + 1) % SLABS) for i in range(SLABS)])
    own = window_sums(True, own_aperture, delay, echo)
    prev = window_sums(False, own_aperture, prev_delay, echo)
    everything = share(own, prev)
    beam, gram = project(
        own_aperture,
        offset.reshape(1, 128),
        depth_slope.reshape(1, 128),
        lateral_tilt.reshape(1, 128),
        everything,
    )
    gram = combine(gram)
    prior = jnp.pad(prior_basis.T, ((0, 32 - RANK), (0, 128 - FRAMES)))
    vmem = pl.BlockSpec(memory_space=VMEM)
    return pl.pallas_call(
        filter_kernel,
        out_shape=jax.ShapeDtypeStruct((1, 4096), F32),
        in_specs=[vmem] * 3,
        out_specs=vmem,
        name="filter",
    )(gram, prior, beam)


def solution(mesh):
    in_specs = (
        P("chan", "vox", None),
        P("chan", "vox"),
        P(),
        P(None, "vox"),
        P(None, "vox"),
        P(None, "vox"),
        P(),
    )
    out_specs = P("vox", "chan")
    return jax.shard_map(body, mesh=mesh, in_specs=in_specs, out_specs=out_specs, check_vma=False)
```

```python
import jax
import jax.numpy as jnp
from jax import lax
from jax.experimental import pallas as pl
from jax.experimental.pallas import tpu as pltpu
from jax.sharding import PartitionSpec as P

MESH = pl.DeviceIdType.MESH
FRAMES = 100
RANK = 30
PAIRS = 50
ROWS = 112
RUN = 16
GROUP = 32
SLABS = 64
SIZE = RUN // 2 * ROWS
VOXELS = 4096
VMEM = pltpu.VMEM
F32 = jnp.float32
BF16 = jnp.bfloat16


def iota(shape, dim):
    return lax.broadcasted_iota(jnp.int32, shape, dim)


def run_start(aperture_ref, slab, group):
    start = jnp.int32(0)
    for b in range(GROUP):
        here = aperture_ref[slab, group * GROUP + b]
        before = aperture_ref[slab, group * GROUP + (b - 1) % GROUP]
        start = start + b * here * (1 - before)
    return start


def window_sums(own, start, gates, delay_ref, echo_ref, moved_ref, rows_ref):
    lane = iota((8, 128), 1)
    sub = iota((8, 128), 0)
    sample = lane & 63
    low = jnp.broadcast_to(delay_ref[0:1, 0:128], (8, 128))
    high = jnp.broadcast_to(delay_ref[0:1, 128:256], (8, 128))

    def pair(i, carry):
        blocks, picks, keeps = [], [], []
        for q in range(2):
            block = lax.rem(start + 2 * i + q, GROUP)
            table = jnp.where(jnp.full((8, 128), block, jnp.int32) < 16, low, high)
            delay = jnp.take_along_axis(table, (block & 15) * 8 + sub, axis=1)
            if own:
                picks.append((lane + delay) & 127)
                keeps.append(sample + delay < 64)
            else:
                picks.append((lane + delay + 64) & 127)
                keeps.append(sample + delay >= 64)
            blocks.append(block)
        for t in range(PAIRS):
            parts = []
            for q in range(2):
                values = echo_ref[blocks[q], :, t * 128 : (t + 1) * 128].astype(F32)
                values = jnp.take_along_axis(values, picks[q], axis=1)
                parts.append(jnp.where(keeps[q], values, 0.0))
            moved_ref[pl.ds(pl.multiple_of(i * 16, 16), 16), t * 128 : (t + 1) * 128] = (
                jnp.concatenate(parts, axis=0).astype(BF16)
            )
        return carry

    lax.fori_loop(0, RUN // 2, pair, 0)
    first = iota((8, 128), 1) < 64
    for c in range(PAIRS // 2):
        sums = jnp.dot(
            gates, moved_ref[:, c * 256 : (c + 1) * 256], preferred_element_type=F32
        )
        for q in range(2):
            p = 2 * c + q
            even = sums[0:8, q * 128 : (q + 1) * 128]
            odd = sums[8:16, q * 128 : (q + 1) * 128]
            rows_ref[pl.ds(2 * p, 8, stride=ROWS), :] = jnp.where(
                first, even, pltpu.roll(odd, 64, 1)
            )
            rows_ref[pl.ds(2 * p + 1, 8, stride=ROWS), :] = jnp.where(
                first, pltpu.roll(even, 64, 1), odd
            )


def sweep(gram, rows):
    product = jnp.dot(rows, gram, precision=lax.Precision.HIGHEST, preferred_element_type=F32)
    normal = lax.dot_general(
        product,
        product,
        (((1,), (1,)), ((), ())),
        precision=lax.Precision.HIGHEST,
        preferred_element_type=F32,
    )
    normal = jnp.concatenate([normal, jnp.zeros((32, 96), F32)], axis=1)
    sub = iota((32, 128), 0)
    scale = jnp.zeros((32, 128), F32)
    for j in range(RANK):
        column = jnp.take_along_axis(normal, jnp.full((32, 128), j, jnp.int32), axis=1)
        pivot = jnp.broadcast_to(column[j : j + 1], (32, 128))
        scale = jnp.where(sub == j, lax.rsqrt(pivot), scale)
        factor = jnp.where(sub > j, column / pivot, 0.0)
        normal = normal - factor * normal[j : j + 1]
        product = product - factor * product[j : j + 1]
    return product * scale


def kernel(
    aperture_smem,
    aperture_ref,
    delay_ref,
    offset_ref,
    slope_ref,
    tilt_ref,
    prior_ref,
    echo_hbm,
    out_ref,
    echo_ref,
    moved_ref,
    rows_ref,
    own_ref,
    prev_ref,
    next_ref,
    prev_delay_ref,
    all_ref,
    table_ref,
    point_ref,
    total_ref,
    beam_ref,
    wide_ref,
    mine_ref,
    got_ref,
    sum_ref,
    gram_ref,
    basis_ref,
    echo_sem,
    ring_send,
    ring_recv,
    peer_send,
    peer_recv,
    send,
    recv,
):
    group = lax.axis_index("chan")
    slab = lax.axis_index("vox")
    before = lax.rem(slab + SLABS - 1, SLABS)
    after = lax.rem(slab + 1, SLABS)
    core = lax.rem(slab, 2)
    chip = slab // 2
    y, z = chip // 8, lax.rem(chip, 8)
    me = group * 2 + core
    around = []
    for d in range(1, 8):
        peer = lax.rem(me + d, 8)
        around.append((peer, (peer // 2, slab - core + lax.rem(peer, 2))))
    along_y = [(group, (lax.rem(y + d, 4) * 8 + z) * 2 + core) for d in range(1, 4)]
    along_z = [(group, (y * 8 + lax.rem(z + d, 8)) * 2 + core) for d in range(1, 8)]
    barrier = pltpu.get_barrier_semaphore()
    places = [(group, before), (group, after)] + [a[1] for a in around] + along_y + along_z
    for place in places:
        pl.semaphore_signal(barrier, inc=1, device_id=place, device_id_type=MESH)
    fetch = pltpu.make_async_copy(echo_hbm, echo_ref, echo_sem)
    fetch.start()

    def copy(src, dst, place, sends, recvs, k):
        return pltpu.make_async_remote_copy(
            src_ref=src,
            dst_ref=dst,
            send_sem=sends.at[k],
            recv_sem=recvs.at[k],
            device_id=place,
            device_id_type=MESH,
        )

    lane1 = iota((1, 128), 1)

    def edges(row):
        last = jnp.where(
            lane1 % GROUP == 0, pltpu.roll(row, 97, 1), pltpu.roll(row, 1, 1)
        )
        return (row * (1 - last) * (lane1 % GROUP)).astype(F32)

    row = aperture_ref[pl.ds(slab, 1), :]
    prev_row = aperture_ref[pl.ds(before, 1), :]
    first_of = edges(row)
    order = iota((RUN, 128), 0)
    order = jnp.where(order < 8, 2 * order, 2 * order - 15)
    member = iota((RUN, 128), 1) // 8 == order

    def gates_of(r):
        count = jnp.sum(
            jnp.where(lane1 // GROUP == group, r.astype(F32), 0.0), axis=1, keepdims=True
        )
        return jnp.where(member & (order.astype(F32) < count), 1.0 / 32, 0.0).astype(BF16)

    rows_ref[...] = jnp.zeros_like(rows_ref)
    lane8 = iota((8, 128), 1)
    sub8 = iota((8, 128), 0)
    depth = (lane8 & 63).astype(F32)
    side = (lane8 >> 6).astype(F32)
    level = iota((16, 128), 0)

    def tables(r, begin, end):
        source = lax.rem(group + r, 4)
        start = jnp.sum(
            jnp.where(lane1 // GROUP == source, first_of, 0.0), axis=1, keepdims=True
        ).astype(jnp.int32)
        bases, tilts = [], []
        for s in range(2):
            pick = source * GROUP + ((jnp.broadcast_to(start, (8, 128)) + sub8 + 8 * s) & 31)

            def values(ref):
                return jnp.take_along_axis(
                    jnp.broadcast_to(ref[0:1, :], (8, 128)), pick, axis=1
                )

            bases.append(values(offset_ref) + values(slope_ref) * depth)
            tilts.append(values(tilt_ref))

        def tile(t, carry):
            lateral = side + (64 * group + 2 * t).astype(F32)
            columns = pl.ds(pl.multiple_of(t * 128, 128), 128)
            for s in range(2):
                position = bases[s] + tilts[s] * lateral
                node = jnp.floor(position)
                right = position - node
                point_ref[s * 24 : s * 24 + 8, :] = node
                point_ref[s * 24 + 8 : s * 24 + 16, :] = 1.0 - right
                point_ref[s * 24 + 16 : s * 24 + 24, :] = right
            for s in range(2):
                for b in range(8):
                    node, left, right = [
                        jnp.concatenate([v, v], axis=0).astype(BF16)
                        for v in [
                            jnp.broadcast_to(
                                point_ref[s * 24 + 8 * k + b : s * 24 + 8 * k + b + 1, :],
                                (8, 128),
                            )
                            for k in range(3)
                        ]
                    ]
                    for k in range(4):
                        at = (level + 16 * k).astype(BF16)
                        past = (level + (16 * k - 1)).astype(BF16)
                        weight = jnp.where(
                            at == node,
                            left,
                            jnp.where(past == node, right, jnp.zeros_like(right)),
                        )
                        base = r * 1024 + (s * 8 + b) * 64 + k * 16
                        table_ref[base : base + 16, columns] = weight
            return carry

        lax.fori_loop(begin, end, tile, 0)

    start = run_start(aperture_smem, slab, group)
    prev_start = run_start(aperture_smem, before, group)
    fetch.wait()
    window_sums(True, start, gates_of(row), delay_ref, echo_ref, moved_ref, rows_ref)
    own_ref[...] = rows_ref[...]
    pl.semaphore_wait(barrier, len(places))

    step = copy(delay_ref, prev_delay_ref, (group, after), ring_send, ring_recv, 0)
    step.start()
    tables(0, 0, 32)
    step.wait()
    window_sums(
        False, prev_start, gates_of(prev_row), prev_delay_ref, echo_ref, moved_ref, rows_ref
    )
    prev_ref[...] = rows_ref[...].astype(BF16)
    step = copy(prev_ref, next_ref, (group, before), ring_send, ring_recv, 1)
    step.start()
    tables(1, 0, 32)
    tables(3, 0, 16)
    step.wait()
    live = jnp.where(slab < SLABS - 1, 1.0, 0.0)
    all_ref[0] = (own_ref[...] + next_ref[...].astype(F32) * live).astype(BF16)
    peers = {
        d: copy(
            all_ref.at[0],
            all_ref.at[4 - d],
            (lax.rem(group + d, 4), slab),
            peer_send,
            peer_recv,
            4 - d,
        )
        for d in range(1, 4)
    }
    for d in (1, 3, 2):
        peers[d].start()
    tables(3, 16, 32)
    tables(2, 0, 32)

    def project(sources, first, last):
        def tile(n, carry):
            columns = pl.ds(pl.multiple_of(n * 256, 256), 256)
            total = None if first else total_ref[:, columns]
            for r in sources:
                for c in range(4):
                    left = jnp.concatenate(
                        [
                            all_ref[r, 2 * c * ROWS : (2 * c + 1) * ROWS, :],
                            all_ref[r, (2 * c + 1) * ROWS : (2 * c + 2) * ROWS, :],
                        ],
                        axis=1,
                    )
                    base = r * 1024 + c * 256
                    part = jnp.dot(
                        left, table_ref[base : base + 256, columns], preferred_element_type=F32
                    )
                    total = part if total is None else total + part
            if not last:
                total_ref[:, columns] = total
                return carry
            high = total.astype(BF16)
            low = (total - high.astype(F32)).astype(BF16)
            blank = jnp.zeros((128 - ROWS, 256), BF16)
            both = jnp.concatenate([high, blank, low, blank], axis=0)
            beam_ref[:, columns] = both
            wide_ref[...] += lax.dot_general(
                both, both, (((1,), (1,)), ((), ())), preferred_element_type=F32
            )
            return carry

        lax.fori_loop(0, VOXELS // 256, tile, 0)

    project((0,), True, False)
    peers[1].wait_recv()
    peers[3].wait_recv()
    project((1, 3), False, False)
    wide_ref[...] = jnp.zeros_like(wide_ref)
    peers[2].wait_recv()
    project((2,), False, True)
    for d in range(1, 4):
        peers[d].wait_send()

    mine_ref[...] = (
        wide_ref[0:128, 0:128]
        + wide_ref[128:256, 0:128]
        + wide_ref[0:128, 128:256]
        + wide_ref[128:256, 128:256]
    )

    def rows(k):
        return pl.ds(pl.multiple_of(k * 16, 16), 16)

    def exchange(copies):
        for c in copies:
            c.start()
        for c in copies:
            c.wait()

    exchange(
        [
            copy(mine_ref.at[rows(peer)], got_ref.at[k], place, send, recv, k)
            for k, (peer, place) in enumerate(around)
        ]
    )
    total = mine_ref[rows(me), :]
    for k in range(7):
        total = total + got_ref[k]
    sum_ref[0] = total
    exchange(
        [
            copy(sum_ref.at[0], got_ref.at[7 + k], place, send, recv, 7 + k)
            for k, place in enumerate(along_y)
        ]
    )
    for k in range(3):
        total = total + got_ref[7 + k]
    sum_ref[1] = total
    exchange(
        [
            copy(sum_ref.at[1], got_ref.at[10 + k], place, send, recv, 10 + k)
            for k, place in enumerate(along_z)
        ]
    )
    for k in range(7):
        total = total + got_ref[10 + k]
    gram_ref[rows(me), :] = total
    exchange(
        [
            copy(gram_ref.at[rows(me)], gram_ref.at[rows(me)], place, send, recv, 17 + k)
            for k, (_, place) in enumerate(around)
        ]
    )

    gram = gram_ref[...]
    basis_ref[...] = jnp.zeros_like(basis_ref)
    basis_ref[0:RANK, 0:FRAMES] = prior_ref[...]
    basis = sweep(gram, basis_ref[...])
    basis = sweep(gram, basis)
    overlap = lax.dot_general(
        basis,
        basis,
        (((0,), (0,)), ((), ())),
        precision=lax.Precision.HIGHEST,
        preferred_element_type=F32,
    )
    keep = jnp.where(iota((128, 128), 0) == iota((128, 128), 1), 1.0, 0.0) - overlap
    high = keep.astype(BF16)
    low = (keep - high.astype(F32)).astype(BF16)
    twice = jnp.concatenate([high, high], axis=1)
    for c in range(VOXELS // 256):
        beam = beam_ref[:, c * 256 : (c + 1) * 256]
        clean = jnp.dot(twice, beam, preferred_element_type=F32)
        clean = clean + jnp.dot(low, beam[0:128], preferred_element_type=F32)
        out_ref[:, c * 256 : (c + 1) * 256] = jnp.sum(
            clean * clean, axis=0, keepdims=True
        ) * (1.0 / FRAMES)


def body(echo_data, delays, aperture, offset, depth_slope, lateral_tilt, prior_basis):
    vmem = pl.BlockSpec(memory_space=VMEM)
    smem = pl.BlockSpec(memory_space=pltpu.SMEM)
    dma = pltpu.SemaphoreType.DMA
    return pl.pallas_call(
        kernel,
        out_shape=jax.ShapeDtypeStruct((1, VOXELS), F32),
        in_specs=[smem] + [vmem] * 6 + [pl.BlockSpec(memory_space=pl.ANY)],
        out_specs=vmem,
        scratch_shapes=[
            VMEM((GROUP, 8, 128 * PAIRS), BF16),
            VMEM((128, 128 * PAIRS), BF16),
            VMEM((SIZE, 128), F32),
            VMEM((SIZE, 128), F32),
            VMEM((SIZE, 128), BF16),
            VMEM((SIZE, 128), BF16),
            VMEM((1, 256), jnp.int32),
            VMEM((4, SIZE, 128), BF16),
            VMEM((4 * RUN * 64, VOXELS), BF16),
            VMEM((48, 128), F32),
            VMEM((ROWS, VOXELS), F32),
            VMEM((256, VOXELS), BF16),
            VMEM((256, 256), F32),
            VMEM((128, 128), F32),
            VMEM((17, 16, 128), F32),
            VMEM((2, 16, 128), F32),
            VMEM((128, 128), F32),
            VMEM((32, 128), F32),
            dma,
            dma((2,)),
            dma((2,)),
            dma((4,)),
            dma((4,)),
            dma((24,)),
            dma((24,)),
        ],
        compiler_params=pltpu.CompilerParams(
            collective_id=0, has_side_effects=True, vmem_limit_bytes=62 * 1024 * 1024
        ),
        name="doppler",
    )(
        aperture.T,
        aperture.T,
        delays.reshape(1, 256),
        offset.reshape(1, 128),
        depth_slope.reshape(1, 128),
        lateral_tilt.reshape(1, 128),
        prior_basis.T,
        echo_data.reshape(GROUP, 8, 128 * PAIRS),
    )


def solution(mesh):
    in_specs = (
        P("chan", "vox", None),
        P("chan", "vox"),
        P(),
        P(None, "vox"),
        P(None, "vox"),
        P(None, "vox"),
        P(),
    )
    out_specs = P("vox", "chan")
    return jax.shard_map(body, mesh=mesh, in_specs=in_specs, out_specs=out_specs, check_vma=False)
```

```python
import jax
import jax.numpy as jnp
from jax import lax
from jax.experimental import pallas as pl
from jax.experimental.pallas import tpu as pltpu
from jax.sharding import PartitionSpec as P

MESH = pl.DeviceIdType.MESH
FRAMES = 100
RANK = 30
PAIRS = 50
ROWS = 104
HALF = 4 * ROWS
STEP = 15
RUN = 16
GROUP = 32
SLABS = 64
SIZE = RUN // 2 * ROWS
VOXELS = 4096
VMEM = pltpu.VMEM
F32 = jnp.float32
BF16 = jnp.bfloat16


def iota(shape, dim):
    return lax.broadcasted_iota(jnp.int32, shape, dim)


def run_start(aperture_ref, slab, group):
    start = jnp.int32(0)
    for b in range(GROUP):
        here = aperture_ref[slab, group * GROUP + b]
        before = aperture_ref[slab, group * GROUP + (b - 1) % GROUP]
        start = start + b * here * (1 - before)
    return start


def window_sums(own, start, gates, delay_ref, echo_ref, moved_ref, rows_ref):
    lane = iota((8, 128), 1)
    sub = iota((8, 128), 0)
    sample = lane & 63
    low = jnp.broadcast_to(delay_ref[0:1, 0:128], (8, 128))
    high = jnp.broadcast_to(delay_ref[0:1, 128:256], (8, 128))

    def blocks(i, carry):
        places, picks, keeps = [], [], []
        for q in range(4):
            block = lax.rem(start + 4 * i + q, GROUP)
            table = jnp.where(jnp.full((8, 128), block, jnp.int32) < 16, low, high)
            delay = jnp.take_along_axis(table, (block & 15) * 8 + sub, axis=1)
            if own:
                picks.append((lane + delay) & 127)
                keeps.append(sample + delay < 64)
            else:
                picks.append((lane + delay + 64) & 127)
                keeps.append(sample + delay >= 64)
            places.append(block)
        for t in range(PAIRS):
            parts = []
            for q in range(4):
                values = echo_ref[places[q], :, t * 128 : (t + 1) * 128].astype(F32)
                values = jnp.take_along_axis(values, picks[q], axis=1)
                parts.append(jnp.where(keeps[q], values, 0.0))
            moved_ref[t, pl.ds(pl.multiple_of(i * 32, 32), 32), :] = jnp.concatenate(
                parts, axis=0
            ).astype(BF16)
        return carry

    lax.fori_loop(0, RUN // 4, blocks, 0)
    first = iota((8, 128), 1) < 64
    for c in range(PAIRS // 2):
        both = jnp.concatenate([moved_ref[2 * c], moved_ref[2 * c + 1]], axis=1)
        sums = jnp.dot(gates, both, preferred_element_type=F32)
        for q in range(2):
            p = 2 * c + q
            even = sums[0:8, q * 128 : (q + 1) * 128]
            odd = sums[8:16, q * 128 : (q + 1) * 128]
            rows_ref[pl.ds(2 * p, 8, stride=ROWS), :] = jnp.where(
                first, even, pltpu.roll(odd, 64, 1)
            )
            rows_ref[pl.ds(2 * p + 1, 8, stride=ROWS), :] = jnp.where(
                first, pltpu.roll(even, 64, 1), odd
            )


def sweep(gram, rows):
    product = jnp.dot(rows, gram, precision=lax.Precision.HIGHEST, preferred_element_type=F32)
    normal = lax.dot_general(
        product,
        product,
        (((1,), (1,)), ((), ())),
        precision=lax.Precision.HIGHEST,
        preferred_element_type=F32,
    )
    normal = jnp.concatenate([normal, jnp.zeros((32, 96), F32)], axis=1)
    sub = iota((32, 128), 0)
    scale = jnp.zeros((32, 128), F32)
    for begin in range(0, RANK, STEP):
        columns = [
            jnp.take_along_axis(normal, jnp.full((32, 128), begin + i, jnp.int32), axis=1)
            for i in range(STEP)
        ]
        for i in range(STEP):
            j = begin + i
            pivot = jnp.broadcast_to(columns[i][j : j + 1], (32, 128))
            factor = jnp.where(sub > j, columns[i] / pivot, 0.0)
            scale = jnp.where(sub == j, lax.rsqrt(pivot), scale)
            for k in range(i + 1, STEP):
                columns[k] = columns[k] - factor * columns[k][j : j + 1]
            normal = normal - factor * normal[j : j + 1]
            product = product - factor * product[j : j + 1]
    return product * scale


def kernel(
    aperture_smem,
    aperture_ref,
    delay_ref,
    offset_ref,
    slope_ref,
    tilt_ref,
    prior_ref,
    echo_hbm,
    out_ref,
    echo_ref,
    moved_ref,
    rows_ref,
    own_ref,
    prev_ref,
    next_ref,
    prev_delay_ref,
    all_ref,
    place_ref,
    point_ref,
    total_ref,
    beam_ref,
    wide_ref,
    mine_ref,
    got_ref,
    sum_ref,
    gram_ref,
    basis_ref,
    echo_sem,
    ring_send,
    ring_recv,
    peer_send,
    peer_recv,
    send,
    recv,
):
    group = lax.axis_index("chan")
    slab = lax.axis_index("vox")
    before = lax.rem(slab + SLABS - 1, SLABS)
    after = lax.rem(slab + 1, SLABS)
    core = lax.rem(slab, 2)
    chip = slab // 2
    y, z = chip // 8, lax.rem(chip, 8)
    me = group * 2 + core
    around = []
    for d in range(1, 8):
        peer = lax.rem(me + d, 8)
        around.append((peer, (peer // 2, slab - core + lax.rem(peer, 2))))
    along_y = [(group, (lax.rem(y + d, 4) * 8 + z) * 2 + core) for d in range(1, 4)]
    along_z = [(group, (y * 8 + lax.rem(z + d, 8)) * 2 + core) for d in range(1, 8)]
    barrier = pltpu.get_barrier_semaphore()
    places = [(group, before), (group, after)] + [a[1] for a in around] + along_y + along_z
    for place in places:
        pl.semaphore_signal(barrier, inc=1, device_id=place, device_id_type=MESH)
    fetch = pltpu.make_async_copy(echo_hbm, echo_ref, echo_sem)
    fetch.start()

    def copy(src, dst, place, sends, recvs, k):
        return pltpu.make_async_remote_copy(
            src_ref=src,
            dst_ref=dst,
            send_sem=sends.at[k],
            recv_sem=recvs.at[k],
            device_id=place,
            device_id_type=MESH,
        )

    lane1 = iota((1, 128), 1)

    def edges(row):
        last = jnp.where(
            lane1 % GROUP == 0, pltpu.roll(row, 97, 1), pltpu.roll(row, 1, 1)
        )
        return (row * (1 - last) * (lane1 % GROUP)).astype(F32)

    row = aperture_ref[pl.ds(slab, 1), :]
    prev_row = aperture_ref[pl.ds(before, 1), :]
    first_of = edges(row)
    order = iota((RUN, 128), 0)
    order = jnp.where(order < 8, 2 * order, 2 * order - 15)
    member = iota((RUN, 128), 1) // 8 == order

    def gates_of(r):
        count = jnp.sum(
            jnp.where(lane1 // GROUP == group, r.astype(F32), 0.0), axis=1, keepdims=True
        )
        return jnp.where(member & (order.astype(F32) < count), 1.0 / 32, 0.0).astype(BF16)

    rows_ref[...] = jnp.zeros_like(rows_ref)
    lane8 = iota((8, 128), 1)
    sub8 = iota((8, 128), 0)
    depth = (lane8 & 63).astype(F32)
    side = (lane8 >> 6).astype(F32)
    level = iota((16, 128), 0)
    levels = [(level + 16 * k).astype(BF16) for k in range(4)]
    pasts = [(level + (16 * k - 1)).astype(BF16) for k in range(4)]

    def place_blocks(r):
        source = lax.rem(group + r, 4)
        start = jnp.sum(
            jnp.where(lane1 // GROUP == source, first_of, 0.0), axis=1, keepdims=True
        ).astype(jnp.int32)
        for s in range(2):
            pick = source * GROUP + ((jnp.broadcast_to(start, (8, 128)) + sub8 + 8 * s) & 31)

            def values(ref):
                return jnp.take_along_axis(
                    jnp.broadcast_to(ref[0:1, :], (8, 128)), pick, axis=1
                )

            tilt = values(tilt_ref)
            lateral = side + (64 * group).astype(F32)
            place_ref[r, s, 0] = values(offset_ref) + values(slope_ref) * depth + tilt * lateral
            place_ref[r, s, 1] = tilt

    pl.semaphore_wait(barrier, len(places))
    step = copy(delay_ref, prev_delay_ref, (group, after), ring_send, ring_recv, 0)
    step.start()
    start = run_start(aperture_smem, slab, group)
    prev_start = run_start(aperture_smem, before, group)
    fetch.wait()
    window_sums(True, start, gates_of(row), delay_ref, echo_ref, moved_ref, rows_ref)
    own_ref[...] = rows_ref[...]
    step.wait()
    window_sums(
        False, prev_start, gates_of(prev_row), prev_delay_ref, echo_ref, moved_ref, rows_ref
    )
    prev_ref[...] = rows_ref[...].astype(BF16)
    step = copy(prev_ref, next_ref, (group, before), ring_send, ring_recv, 1)
    step.start()
    for r in range(4):
        place_blocks(r)
    blank = jnp.zeros((128 - ROWS, 128), BF16)
    for t in range(VOXELS // 128):
        beam_ref[t, ROWS:128, :] = blank
        beam_ref[t, 128 + ROWS : 256, :] = blank
    live = jnp.where(slab < SLABS - 1, 1.0, 0.0)
    step.wait()
    all_ref[0] = (own_ref[...] + next_ref[...].astype(F32) * live).astype(BF16)
    right, left = (lax.rem(group + 1, 4), slab), (lax.rem(group + 3, 4), slab)
    upper, lower = pl.ds(0, HALF), pl.ds(HALF, HALF)

    def pass_on(source, target, part, place, k):
        return copy(
            all_ref.at[source, part], all_ref.at[target, part], place, peer_send, peer_recv, k
        )

    own_copies = [
        pass_on(0, 3, upper, right, 0),
        pass_on(0, 1, lower, left, 1),
        pass_on(0, 3, lower, right, 2),
        pass_on(0, 1, upper, left, 3),
    ]
    far_copies = [pass_on(3, 2, upper, right, 4), pass_on(1, 2, lower, left, 5)]
    for c in own_copies:
        c.start()
    def weights_of(at, b):
        node, left, right = [
            jnp.broadcast_to(point_ref[at + 8 * k + b : at + 8 * k + b + 1, :], (16, 128)).astype(
                BF16
            )
            for k in range(3)
        ]
        return jnp.concatenate(
            [
                jnp.where(
                    levels[k] == node,
                    left,
                    jnp.where(pasts[k] == node, right, jnp.zeros_like(right)),
                )
                for k in range(4)
            ],
            axis=0,
        )

    def project(units, first, last):
        def tile(i, carry):
            at = 0
            for v in range(2):
                for r, s in units:
                    base, tilt = place_ref[r, s, 0], place_ref[r, s, 1]
                    for u in range(2):
                        position = base + tilt * (8 * i + 4 * v + 2 * u).astype(F32)
                        node = jnp.floor(position)
                        right = position - node
                        point_ref[at : at + 8, :] = node
                        point_ref[at + 8 : at + 16, :] = 1.0 - right
                        point_ref[at + 16 : at + 24, :] = right
                        at += 24
            at = 0
            for v in range(2):
                n = 2 * i + v
                columns = pl.ds(pl.multiple_of(n * 256, 256), 256)
                total = None if first else total_ref[:, columns]
                for r, s in units:
                    for c in range(2):
                        weights = jnp.concatenate(
                            [
                                jnp.concatenate(
                                    [weights_of(at, b), weights_of(at + 24, b)], axis=1
                                )
                                for b in range(4 * c, 4 * c + 4)
                            ],
                            axis=0,
                        )
                        m = 4 * s + 2 * c
                        blocks = jnp.concatenate(
                            [
                                all_ref[r, m * ROWS : (m + 1) * ROWS, :],
                                all_ref[r, (m + 1) * ROWS : (m + 2) * ROWS, :],
                            ],
                            axis=1,
                        )
                        part = jnp.dot(blocks, weights, preferred_element_type=F32)
                        total = part if total is None else total + part
                    at += 48
                if not last:
                    total_ref[:, columns] = total
                    continue
                high = total.astype(BF16)
                low = (total - high.astype(F32)).astype(BF16)
                for q in range(2):
                    lanes = slice(q * 128, q * 128 + 128)
                    beam_ref[2 * n + q, 0:ROWS, :] = high[:, lanes]
                    beam_ref[2 * n + q, 128 : 128 + ROWS, :] = low[:, lanes]
            return carry

        lax.fori_loop(0, VOXELS // 512, tile, 0)

    project(((0, 0), (0, 1)), True, False)
    for k in range(2):
        own_copies[k].wait_recv()
        far_copies[k].start()
    project(((3, 0), (1, 1)), False, False)
    for k in range(2, 4):
        own_copies[k].wait_recv()
    project(((3, 1), (1, 0)), False, False)
    for c in far_copies:
        c.wait_recv()
    project(((2, 0), (2, 1)), False, True)
    for c in own_copies + far_copies:
        c.wait_send()
    wide_ref[...] = jnp.zeros_like(wide_ref)

    def square(i, carry):
        part = jnp.concatenate([beam_ref[8 * i + k] for k in range(8)], axis=1)
        wide_ref[...] += lax.dot_general(
            part, part[0:128], (((1,), (1,)), ((), ())), preferred_element_type=F32
        )
        return carry

    lax.fori_loop(0, 4, square, 0)
    cross = wide_ref[128:256, :]
    mine_ref[...] = wide_ref[0:128, :] + cross + cross.T

    def rows(k):
        return pl.ds(pl.multiple_of(k * 16, 16), 16)

    def exchange(copies):
        for c in copies:
            c.start()
        for c in copies:
            c.wait()

    exchange(
        [
            copy(mine_ref.at[rows(peer)], got_ref.at[k], place, send, recv, k)
            for k, (peer, place) in enumerate(around)
        ]
    )
    total = mine_ref[rows(me), :]
    for k in range(7):
        total = total + got_ref[k]
    sum_ref[0] = total
    exchange(
        [
            copy(sum_ref.at[0], got_ref.at[7 + k], place, send, recv, 7 + k)
            for k, place in enumerate(along_y)
        ]
    )
    for k in range(3):
        total = total + got_ref[7 + k]
    sum_ref[1] = total
    exchange(
        [
            copy(sum_ref.at[1], got_ref.at[10 + k], place, send, recv, 10 + k)
            for k, place in enumerate(along_z)
        ]
    )
    for k in range(7):
        total = total + got_ref[10 + k]
    gram_ref[rows(me), :] = total
    exchange(
        [
            copy(gram_ref.at[rows(me)], gram_ref.at[rows(me)], place, send, recv, 17 + k)
            for k, (_, place) in enumerate(around)
        ]
    )

    gram = gram_ref[...]
    basis_ref[...] = jnp.zeros_like(basis_ref)
    basis_ref[0:RANK, 0:FRAMES] = prior_ref[...]
    basis = sweep(gram, basis_ref[...])
    basis = sweep(gram, basis)
    overlap = lax.dot_general(
        basis,
        basis,
        (((0,), (0,)), ((), ())),
        precision=lax.Precision.HIGHEST,
        preferred_element_type=F32,
    )
    keep = jnp.where(iota((128, 128), 0) == iota((128, 128), 1), 1.0, 0.0) - overlap
    high = keep.astype(BF16)
    low = (keep - high.astype(F32)).astype(BF16)
    twice = jnp.concatenate([high, high], axis=1)
    for c in range(VOXELS // 256):
        beam = jnp.concatenate([beam_ref[2 * c], beam_ref[2 * c + 1]], axis=1)
        clean = jnp.dot(twice, beam, preferred_element_type=F32)
        clean = clean + jnp.dot(low, beam[0:128], preferred_element_type=F32)
        out_ref[:, c * 256 : (c + 1) * 256] = jnp.sum(clean * clean, axis=0, keepdims=True)


def body(echo_data, delays, aperture, offset, depth_slope, lateral_tilt, prior_basis):
    vmem = pl.BlockSpec(memory_space=VMEM)
    smem = pl.BlockSpec(memory_space=pltpu.SMEM)
    dma = pltpu.SemaphoreType.DMA
    squares = pl.pallas_call(
        kernel,
        out_shape=jax.ShapeDtypeStruct((1, VOXELS), F32),
        in_specs=[smem] + [vmem] * 6 + [pl.BlockSpec(memory_space=pl.ANY)],
        out_specs=vmem,
        scratch_shapes=[
            VMEM((GROUP, 8, 128 * PAIRS), BF16),
            VMEM((PAIRS, 128, 128), BF16),
            VMEM((SIZE, 128), F32),
            VMEM((SIZE, 128), F32),
            VMEM((SIZE, 128), BF16),
            VMEM((SIZE, 128), BF16),
            VMEM((1, 256), jnp.int32),
            VMEM((4, SIZE, 128), BF16),
            VMEM((4, 2, 2, 8, 128), F32),
            VMEM((192, 128), F32),
            VMEM((ROWS, VOXELS), F32),
            VMEM((VOXELS // 128, 256, 128), BF16),
            VMEM((256, 128), F32),
            VMEM((128, 128), F32),
            VMEM((17, 16, 128), F32),
            VMEM((2, 16, 128), F32),
            VMEM((128, 128), F32),
            VMEM((32, 128), F32),
            dma,
            dma((2,)),
            dma((2,)),
            dma((6,)),
            dma((6,)),
            dma((24,)),
            dma((24,)),
        ],
        compiler_params=pltpu.CompilerParams(
            collective_id=0, has_side_effects=True, vmem_limit_bytes=62 * 1024 * 1024
        ),
        name="doppler",
    )(
        aperture.T,
        aperture.T,
        delays.reshape(1, 256),
        offset.reshape(1, 128),
        depth_slope.reshape(1, 128),
        lateral_tilt.reshape(1, 128),
        prior_basis.T,
        echo_data.reshape(GROUP, 8, 128 * PAIRS),
    )
    return squares / FRAMES


def solution(mesh):
    in_specs = (
        P("chan", "vox", None),
        P("chan", "vox"),
        P(),
        P(None, "vox"),
        P(None, "vox"),
        P(None, "vox"),
        P(),
    )
    out_specs = P("vox", "chan")
    return jax.shard_map(body, mesh=mesh, in_specs=in_specs, out_specs=out_specs, check_vma=False)
```

```python
import jax
import jax.numpy as jnp
from jax import lax
from jax.experimental import pallas as pl
from jax.experimental.pallas import tpu as pltpu
from jax.sharding import PartitionSpec as P

MESH = pl.DeviceIdType.MESH
FRAMES = 100
RANK = 30
PAIRS = 50
ROWS = 104
HALF = 4 * ROWS
SIDE = ROWS // 2
STEP = 15
RUN = 16
GROUP = 32
SLABS = 64
SIZE = RUN // 2 * ROWS
VOXELS = 4096
VMEM = pltpu.VMEM
F32 = jnp.float32
BF16 = jnp.bfloat16


def iota(shape, dim):
    return lax.broadcasted_iota(jnp.int32, shape, dim)


def run_start(run_ref, which, group):
    start = jnp.int32(0)
    before = run_ref[which, group * GROUP + GROUP - 1]
    for b in range(GROUP):
        here = run_ref[which, group * GROUP + b]
        start = start + b * here * (1 - before)
        before = here
    return start


def window_sums(own, half, start, gates, delay_ref, echo_ref, moved_ref, rows_ref):
    lane = iota((8, 128), 1)
    sub = iota((8, 128), 0)
    sample = lane & 63
    low = jnp.broadcast_to(delay_ref[0:1, 0:128], (8, 128))
    high = jnp.broadcast_to(delay_ref[0:1, 128:256], (8, 128))

    def blocks(i, carry):
        places, picks, keeps = [], [], []
        for q in range(4):
            block = lax.rem(start + 8 * half + 4 * i + q, GROUP)
            table = jnp.where(jnp.full((8, 128), block, jnp.int32) < 16, low, high)
            delay = jnp.take_along_axis(table, (block & 15) * 8 + sub, axis=1)
            if own:
                picks.append((lane + delay) & 127)
                keeps.append(sample + delay < 64)
            else:
                picks.append((lane + delay + 64) & 127)
                keeps.append(sample + delay >= 64)
            places.append(block)
        for t in range(PAIRS):
            parts = []
            for q in range(4):
                values = echo_ref[places[q], :, t * 128 : (t + 1) * 128].astype(F32)
                values = jnp.take_along_axis(values, picks[q], axis=1)
                parts.append(jnp.where(keeps[q], values, 0.0))
            moved_ref[t, pl.ds(pl.multiple_of(i * 32, 32), 32), :] = jnp.concatenate(
                parts, axis=0
            ).astype(BF16)
        return carry

    lax.fori_loop(0, RUN // 8, blocks, 0)
    first = lane < 64
    even_frame = (sub & 1) == 0
    for c in range(PAIRS // 2):
        both = jnp.concatenate([moved_ref[2 * c], moved_ref[2 * c + 1]], axis=1)
        sums = jnp.dot(gates, both, preferred_element_type=F32)
        for q in range(2):
            even = sums[0:8, q * 128 : (q + 1) * 128]
            odd = sums[8:16, q * 128 : (q + 1) * 128]
            rows_ref[pl.ds(2 * c + q, 8, stride=SIDE), :] = jnp.where(
                first,
                jnp.where(even_frame, even, pltpu.roll(even, 64, 1)),
                jnp.where(even_frame, pltpu.roll(odd, 64, 1), odd),
            )


def sweep(gram, rows):
    product = jnp.dot(rows, gram, precision=lax.Precision.HIGHEST, preferred_element_type=F32)
    normal = lax.dot_general(
        product,
        product,
        (((1,), (1,)), ((), ())),
        precision=lax.Precision.HIGHEST,
        preferred_element_type=F32,
    )
    normal = jnp.concatenate([normal, jnp.zeros((32, 96), F32)], axis=1)
    sub = iota((32, 128), 0)
    scale = jnp.zeros((32, 128), F32)
    for begin in range(0, RANK, STEP):
        columns = [
            jnp.take_along_axis(normal, jnp.full((32, 128), begin + i, jnp.int32), axis=1)
            for i in range(STEP)
        ]
        for i in range(STEP):
            j = begin + i
            pivot = jnp.broadcast_to(columns[i][j : j + 1], (32, 128))
            factor = jnp.where(sub > j, columns[i] / pivot, 0.0)
            scale = jnp.where(sub == j, lax.rsqrt(pivot), scale)
            for k in range(i + 1, STEP):
                columns[k] = columns[k] - factor * columns[k][j : j + 1]
            normal = normal - factor * normal[j : j + 1]
            product = product - factor * product[j : j + 1]
    return product * scale


def kernel(
    aperture_hbm,
    delay_hbm,
    offset_hbm,
    slope_hbm,
    tilt_hbm,
    prior_hbm,
    echo_hbm,
    out_ref,
    run_ref,
    aperture_ref,
    delay_ref,
    offset_ref,
    slope_ref,
    tilt_ref,
    prior_ref,
    echo_ref,
    moved_ref,
    rows_ref,
    own_ref,
    prev_ref,
    next_ref,
    prev_delay_ref,
    all_ref,
    place_ref,
    point_ref,
    total_ref,
    beam_ref,
    wide_ref,
    mine_ref,
    got_ref,
    sum_ref,
    gram_ref,
    basis_ref,
    power_ref,
    input_sem,
    ring_send,
    ring_recv,
    peer_send,
    peer_recv,
    send,
    recv,
):
    group = lax.axis_index("chan")
    slab = lax.axis_index("vox")
    before = lax.rem(slab + SLABS - 1, SLABS)
    after = lax.rem(slab + 1, SLABS)
    core = lax.rem(slab, 2)
    chip = slab // 2
    y, z = chip // 8, lax.rem(chip, 8)
    me = y * 8 + group * 2 + core
    around = []
    for dy in range(4):
        row_y = lax.rem(y + dy, 4)
        for d in range(8):
            if dy == 0 and d == 0:
                continue
            inner = lax.rem(group * 2 + core + d, 8)
            around.append(
                (row_y * 8 + inner, (inner // 2, (row_y * 8 + z) * 2 + lax.rem(inner, 2)))
            )
    along_z = [(group, (y * 8 + lax.rem(z + d, 8)) * 2 + core) for d in range(1, 8)]
    inputs = [
        pltpu.make_async_copy(source, target, input_sem.at[k])
        for k, (source, target) in enumerate(
            [
                (aperture_hbm.at[pl.ds(slab, 1), :], run_ref.at[pl.ds(0, 1), :]),
                (aperture_hbm.at[pl.ds(before, 1), :], run_ref.at[pl.ds(1, 1), :]),
                (delay_hbm, delay_ref),
                (aperture_hbm, aperture_ref),
                (offset_hbm, offset_ref),
                (slope_hbm, slope_ref),
                (tilt_hbm, tilt_ref),
                (prior_hbm, prior_ref),
                (echo_hbm, echo_ref),
            ]
        )
    ]
    for c in inputs:
        c.start()
    barrier = pltpu.get_barrier_semaphore()
    places = along_z + [a[1] for a in around[::-1]] + [(group, before), (group, after)]
    for place in places:
        pl.semaphore_signal(barrier, inc=1, device_id=place, device_id_type=MESH)
    for c in inputs[:-1]:
        c.wait()

    def copy(src, dst, place, sends, recvs, k):
        return pltpu.make_async_remote_copy(
            src_ref=src,
            dst_ref=dst,
            send_sem=sends.at[k],
            recv_sem=recvs.at[k],
            device_id=place,
            device_id_type=MESH,
        )

    lane1 = iota((1, 128), 1)

    def edges(row):
        last = jnp.where(
            lane1 % GROUP == 0, pltpu.roll(row, 97, 1), pltpu.roll(row, 1, 1)
        )
        return (row * (1 - last) * (lane1 % GROUP)).astype(F32)

    row = aperture_ref[pl.ds(slab, 1), :]
    prev_row = aperture_ref[pl.ds(before, 1), :]
    first_of = edges(row)
    order = iota((16, 64), 0)
    order = jnp.where(order < 8, 2 * (order // 2), 2 * (order // 2) - 7)
    member = iota((16, 64), 1) // 8 == order

    def gates_of(r, half):
        count = jnp.sum(
            jnp.where(lane1 // GROUP == group, r.astype(F32), 0.0), axis=1, keepdims=True
        )
        return jnp.where(
            member & ((order + 8 * half).astype(F32) < count), 1.0 / 32, 0.0
        ).astype(BF16)

    rows_ref[...] = jnp.zeros_like(rows_ref)
    lane8 = iota((8, 128), 1)
    sub8 = iota((8, 128), 0)
    depth = (lane8 & 15).astype(F32)
    side = (lane8 >> 4).astype(F32)
    level = iota((16, 128), 0)
    levels = [(level + 16 * k).astype(BF16) for k in range(4)]
    pasts = [(level + (16 * k - 1)).astype(BF16) for k in range(4)]

    def place_blocks(r):
        source = lax.rem(group + r, 4)
        start = jnp.sum(
            jnp.where(lane1 // GROUP == source, first_of, 0.0), axis=1, keepdims=True
        ).astype(jnp.int32)
        for s in range(2):
            pick = source * GROUP + ((jnp.broadcast_to(start, (8, 128)) + sub8 + 8 * s) & 31)

            def values(ref):
                return jnp.take_along_axis(
                    jnp.broadcast_to(ref[0:1, :], (8, 128)), pick, axis=1
                )

            slope, tilt = values(slope_ref), values(tilt_ref)
            lateral = side + (64 * group).astype(F32)
            place_ref[r, s, 0] = values(offset_ref) + slope * depth + tilt * lateral
            place_ref[r, s, 1] = tilt * 8.0
            place_ref[r, s, 2] = slope * 16.0

    start = run_start(run_ref, 0, group)
    prev_start = run_start(run_ref, 1, group)
    inputs[-1].wait()

    def own_half(half):
        window_sums(
            True, half, start, gates_of(row, half), delay_ref, echo_ref, moved_ref, rows_ref
        )
        own_ref[half] = rows_ref[...]

    own_half(0)
    pl.semaphore_wait(barrier, len(places))
    step = copy(delay_ref, prev_delay_ref, (group, after), ring_send, ring_recv, 0)
    has_before, has_after = slab > 0, slab < SLABS - 1
    pl.when(has_after)(step.start)
    own_half(1)

    @pl.when(jnp.logical_not(has_before))
    def _():
        prev_delay_ref[...] = jnp.zeros_like(prev_delay_ref)

    @pl.when(jnp.logical_not(has_after))
    def _():
        next_ref[...] = jnp.zeros_like(next_ref)

    pl.when(has_before)(step.wait_recv)
    steps = []
    for half in range(2):
        gates = gates_of(prev_row, half)
        window_sums(
            False, half, prev_start, gates, prev_delay_ref, echo_ref, moved_ref, rows_ref
        )
        prev_ref[half] = rows_ref[...].astype(BF16)
        steps.append(
            copy(
                prev_ref.at[half],
                next_ref.at[half],
                (group, before),
                ring_send,
                ring_recv,
                1 + half,
            )
        )
        pl.when(has_before)(steps[half].start)
    for r in range(4):
        place_blocks(r)
    blank = jnp.zeros((128 - ROWS, 128), BF16)
    for t in range(VOXELS // 128):
        beam_ref[t, ROWS:128, :] = blank
        beam_ref[t, 128 + ROWS : 256, :] = blank
    right, left = (lax.rem(group + 1, 4), slab), (lax.rem(group + 3, 4), slab)

    def pass_on(source, target, begin, size, place, k):
        part = pl.ds(begin, size)
        return copy(
            all_ref.at[source, part], all_ref.at[target, part], place, peer_send, peer_recv, k
        )

    near_copies, far_copies = [], []
    for half in range(2):
        begin = half * HALF
        near_copies.append(
            [
                pass_on(0, 3, begin, HALF, right, 4 * half),
                pass_on(0, 1, begin, HALF, left, 4 * half + 1),
            ]
        )
        far_copies.append(
            [
                pass_on(3, 2, begin, HALF // 2, right, 4 * half + 2),
                pass_on(1, 2, begin + HALF // 2, HALF // 2, left, 4 * half + 3),
            ]
        )
    for half in range(2):
        pl.when(has_after)(steps[half].wait_recv)
        all_ref[0, half * HALF : (half + 1) * HALF, :] = (
            own_ref[half] + next_ref[half].astype(F32)
        ).astype(BF16)
        for c in near_copies[half]:
            c.start()

    def weights_of(at, b, skip):
        node, left, right = [
            jnp.broadcast_to(point_ref[at + 8 * k + b : at + 8 * k + b + 1, :], (16, 128)).astype(
                BF16
            )
            for k in range(3)
        ]
        none = jnp.zeros_like(right)
        return jnp.concatenate(
            [
                none
                if k == skip
                else jnp.where(
                    levels[k] == node, left, jnp.where(pasts[k] == node, right, none)
                )
                for k in range(4)
            ],
            axis=0,
        )

    near = 4 - group

    def project(units, first, last):
        lax.fori_loop(0, near, project_tile(units, first, last, 3), 0)
        lax.fori_loop(near, 4, project_tile(units, first, last, 0), 0)

    def project_tile(units, first, last, skip):
        def tile(i, carry):
            at = 0
            for v in range(4):
                for r, s in units:
                    base = place_ref[r, s, 0] + place_ref[r, s, 2] * i.astype(F32)
                    for u in range(2):
                        position = base + place_ref[r, s, 1] * float(2 * v + u)
                        node = jnp.floor(position)
                        right = position - node
                        point_ref[at : at + 8, :] = node
                        point_ref[at + 8 : at + 16, :] = 1.0 - right
                        point_ref[at + 16 : at + 24, :] = right
                        at += 24
            at = 0
            for v in range(4):
                n = 4 * i + v
                columns = pl.ds(pl.multiple_of(n * 256, 256), 256)
                total = None if first else total_ref[:, columns]
                for r, s in units:
                    for c in range(2):
                        weights = jnp.concatenate(
                            [
                                jnp.concatenate(
                                    [weights_of(at, b, skip), weights_of(at + 24, b, skip)],
                                    axis=1,
                                )
                                for b in range(4 * c, 4 * c + 4)
                            ],
                            axis=0,
                        )
                        m = 4 * s + 2 * c
                        blocks = jnp.concatenate(
                            [
                                all_ref[r, m * ROWS : (m + 1) * ROWS, :],
                                all_ref[r, (m + 1) * ROWS : (m + 2) * ROWS, :],
                            ],
                            axis=1,
                        )
                        part = jnp.dot(blocks, weights, preferred_element_type=F32)
                        total = part if total is None else total + part
                    at += 48
                if not last:
                    total_ref[:, columns] = total
                    continue
                high = total.astype(BF16)
                low = (total - high.astype(F32)).astype(BF16)
                for q in range(2):
                    lanes = slice(q * 128, q * 128 + 128)
                    beam_ref[2 * n + q, 0:ROWS, :] = high[:, lanes]
                    beam_ref[2 * n + q, 128 : 128 + ROWS, :] = low[:, lanes]
            return carry

        return tile

    project(((0, 0), (0, 1)), True, False)
    for half in range(2):
        for k in range(2):
            near_copies[half][k].wait_recv()
            far_copies[half][k].start()
        project(((3, half), (1, half)), False, False)
    for c in far_copies[0] + far_copies[1]:
        c.wait_recv()
    project(((2, 0), (2, 1)), False, True)
    pl.when(has_after)(step.wait_send)
    for half in range(2):
        pl.when(has_before)(steps[half].wait_send)
        for c in near_copies[half] + far_copies[half]:
            c.wait_send()
    wide_ref[...] = jnp.zeros_like(wide_ref)

    def square(i, carry):
        part = jnp.concatenate([beam_ref[8 * i + k] for k in range(8)], axis=1)
        wide_ref[...] += lax.dot_general(
            part, part[0:128], (((1,), (1,)), ((), ())), preferred_element_type=F32
        )
        return carry

    lax.fori_loop(0, 4, square, 0)
    cross = wide_ref[128:256, :]
    gram = wide_ref[0:128, :] + cross + cross.T
    for k in range(32):
        mine_ref[k] = gram[4 * k : 4 * k + 4]

    def exchange(copies):
        for c in copies:
            c.start()
        for c in copies:
            c.wait()

    exchange(
        [
            copy(mine_ref.at[peer], got_ref.at[k], place, send, recv, k)
            for k, (peer, place) in enumerate(around)
        ]
    )
    total = mine_ref[me]
    for k in range(31):
        total = total + got_ref[k]
    sum_ref[...] = total
    exchange(
        [
            copy(sum_ref, got_ref.at[31 + k], place, send, recv, 31 + k)
            for k, place in enumerate(along_z)
        ]
    )
    for k in range(7):
        total = total + got_ref[31 + k]
    gram_ref[me] = total
    exchange(
        [
            copy(gram_ref.at[me], gram_ref.at[me], place, send, recv, 38 + k)
            for k, (_, place) in enumerate(around)
        ]
    )

    gram = jnp.concatenate([gram_ref[k] for k in range(32)], axis=0)
    basis_ref[...] = jnp.zeros_like(basis_ref)
    basis_ref[0:RANK, 0:FRAMES] = prior_ref[...]
    lane = iota((32, 128), 1)
    odd = (lane >= SIDE).astype(jnp.int32)
    frame = 2 * (lane - SIDE * odd) + odd
    basis = jnp.take_along_axis(basis_ref[...], jnp.minimum(frame, 127), axis=1)
    basis = jnp.where(frame < FRAMES, basis, 0.0)
    basis = sweep(gram, basis)
    basis = sweep(gram, basis)
    overlap = lax.dot_general(
        basis,
        basis,
        (((0,), (0,)), ((), ())),
        precision=lax.Precision.HIGHEST,
        preferred_element_type=F32,
    )
    keep = jnp.where(iota((128, 128), 0) == iota((128, 128), 1), 1.0, 0.0) - overlap
    high = keep.astype(BF16)
    low = (keep - high.astype(F32)).astype(BF16)
    twice = jnp.concatenate([high, high], axis=1)
    for c in range(VOXELS // 256):
        beam = jnp.concatenate([beam_ref[2 * c], beam_ref[2 * c + 1]], axis=1)
        clean = jnp.dot(twice, beam, preferred_element_type=F32)
        clean = clean + jnp.dot(low, beam[0:128], preferred_element_type=F32)
        power = jnp.sum(clean * clean, axis=0, keepdims=True)
        power_ref[2 * c : 2 * c + 1, :] = power[:, 0:128]
        power_ref[2 * c + 1 : 2 * c + 2, :] = power[:, 128:256]
    pick = (2 * (sub8 & 3) + (lane8 >> 6)) * 16 + (lane8 & 15)
    quarter = (lane8 >> 4) & 3
    for p in range(4):
        rows = None
        for q in range(4):
            one = jnp.broadcast_to(power_ref[8 * q + 2 * p : 8 * q + 2 * p + 1, :], (8, 128))
            two = jnp.broadcast_to(power_ref[8 * q + 2 * p + 1 : 8 * q + 2 * p + 2, :], (8, 128))
            got = jnp.take_along_axis(jnp.where(sub8 < 4, one, two), pick, axis=1)
            rows = got if rows is None else jnp.where(quarter == q, got, rows)
        out_ref[8 * p : 8 * p + 8, :] = rows


def body(echo_data, delays, aperture, offset, depth_slope, lateral_tilt, prior_basis):
    vmem = pl.BlockSpec(memory_space=VMEM)
    dma = pltpu.SemaphoreType.DMA
    squares = pl.pallas_call(
        kernel,
        out_shape=VMEM((VOXELS // 128, 128), F32),
        in_specs=[pl.BlockSpec(memory_space=pl.ANY)] * 7,
        out_specs=vmem,
        scratch_shapes=[
            pltpu.SMEM((2, 128), jnp.int32),
            VMEM((SLABS, 128), jnp.int32),
            VMEM((1, 256), jnp.int32),
            VMEM((1, 128), F32),
            VMEM((1, 128), F32),
            VMEM((1, 128), F32),
            VMEM((RANK, FRAMES), F32),
            VMEM((GROUP, 8, 128 * PAIRS), BF16),
            VMEM((PAIRS, 64, 128), BF16),
            VMEM((HALF, 128), F32),
            VMEM((2, HALF, 128), F32),
            VMEM((2, HALF, 128), BF16),
            VMEM((2, HALF, 128), BF16),
            VMEM((1, 256), jnp.int32),
            VMEM((4, SIZE, 128), BF16),
            VMEM((4, 2, 3, 8, 128), F32),
            VMEM((384, 128), F32),
            VMEM((ROWS, VOXELS), F32),
            VMEM((VOXELS // 128, 256, 128), BF16),
            VMEM((256, 128), F32),
            VMEM((32, 4, 128), F32),
            VMEM((38, 4, 128), F32),
            VMEM((4, 128), F32),
            VMEM((32, 4, 128), F32),
            VMEM((32, 128), F32),
            VMEM((VOXELS // 128, 128), F32),
            dma((9,)),
            dma((3,)),
            dma((3,)),
            dma((8,)),
            dma((8,)),
            dma((69,)),
            dma((69,)),
        ],
        compiler_params=pltpu.CompilerParams(
            collective_id=0, has_side_effects=True, vmem_limit_bytes=62 * 1024 * 1024
        ),
        name="doppler",
    )(
        aperture.T,
        delays.reshape(1, 256),
        offset.reshape(1, 128),
        depth_slope.reshape(1, 128),
        lateral_tilt.reshape(1, 128),
        prior_basis.T,
        echo_data.reshape(GROUP, 8, 128 * PAIRS),
    )
    return squares.reshape(1, VOXELS) / FRAMES


def solution(mesh):
    in_specs = (
        P("chan", "vox", None),
        P("chan", "vox"),
        P(),
        P(None, "vox"),
        P(None, "vox"),
        P(None, "vox"),
        P(),
    )
    out_specs = P("vox", "chan")
    return jax.shard_map(body, mesh=mesh, in_specs=in_specs, out_specs=out_specs, check_vma=False)
```

```python
import jax
import jax.numpy as jnp
from jax import lax
from jax.experimental import pallas as pl
from jax.experimental.pallas import tpu as pltpu
from jax.sharding import PartitionSpec as P

MESH = pl.DeviceIdType.MESH
FRAMES = 100
RANK = 30
PAIRS = 50
ROWS = 104
HALF = 4 * ROWS
SIDE = ROWS // 2
STEP = 15
RUN = 16
GROUP = 32
SLABS = 64
SIZE = RUN // 2 * ROWS
VOXELS = 4096
VMEM = pltpu.VMEM
F32 = jnp.float32
BF16 = jnp.bfloat16


def iota(shape, dim):
    return lax.broadcasted_iota(jnp.int32, shape, dim)


def run_start(run_ref, which, group):
    start = jnp.int32(0)
    before = run_ref[which, group * GROUP + GROUP - 1]
    for b in range(GROUP):
        here = run_ref[which, group * GROUP + b]
        start = start + b * here * (1 - before)
        before = here
    return start


def window_sums(own, half, start, gates, delay_ref, echo_ref, moved_ref, rows_ref):
    lane = iota((8, 128), 1)
    sub = iota((8, 128), 0)
    sample = lane & 63
    low = jnp.broadcast_to(delay_ref[0:1, 0:128], (8, 128))
    high = jnp.broadcast_to(delay_ref[0:1, 128:256], (8, 128))

    def blocks(i, carry):
        places, picks, keeps = [], [], []
        for q in range(4):
            block = lax.rem(start + 8 * half + 4 * i + q, GROUP)
            table = jnp.where(jnp.full((8, 128), block, jnp.int32) < 16, low, high)
            delay = jnp.take_along_axis(table, (block & 15) * 8 + sub, axis=1)
            if own:
                picks.append((lane + delay) & 127)
                keeps.append(sample + delay < 64)
            else:
                picks.append((lane + delay + 64) & 127)
                keeps.append(sample + delay >= 64)
            places.append(block)
        for t in range(PAIRS):
            parts = []
            for q in range(4):
                values = echo_ref[places[q], :, t * 128 : (t + 1) * 128].astype(F32)
                values = jnp.take_along_axis(values, picks[q], axis=1)
                parts.append(jnp.where(keeps[q], values, 0.0))
            moved_ref[t, pl.ds(pl.multiple_of(i * 32, 32), 32), :] = jnp.concatenate(
                parts, axis=0
            ).astype(BF16)
        return carry

    lax.fori_loop(0, RUN // 8, blocks, 0)
    first = lane < 64
    even_frame = (sub & 1) == 0
    for c in range(PAIRS // 2):
        both = jnp.concatenate([moved_ref[2 * c], moved_ref[2 * c + 1]], axis=1)
        sums = jnp.dot(gates, both, preferred_element_type=F32)
        for q in range(2):
            even = sums[0:8, q * 128 : (q + 1) * 128]
            odd = sums[8:16, q * 128 : (q + 1) * 128]
            rows_ref[pl.ds(2 * c + q, 8, stride=SIDE), :] = jnp.where(
                first,
                jnp.where(even_frame, even, pltpu.roll(even, 64, 1)),
                jnp.where(even_frame, pltpu.roll(odd, 64, 1), odd),
            )


def sweep(gram, rows):
    product = jnp.dot(rows, gram, precision=lax.Precision.HIGHEST, preferred_element_type=F32)
    normal = lax.dot_general(
        product,
        product,
        (((1,), (1,)), ((), ())),
        precision=lax.Precision.HIGHEST,
        preferred_element_type=F32,
    )
    normal = jnp.concatenate([normal, jnp.zeros((32, 96), F32)], axis=1)
    sub = iota((32, 128), 0)
    scale = jnp.zeros((32, 128), F32)
    for begin in range(0, RANK, STEP):
        columns = [
            jnp.take_along_axis(normal, jnp.full((32, 128), begin + i, jnp.int32), axis=1)
            for i in range(STEP)
        ]
        for i in range(STEP):
            j = begin + i
            pivot = jnp.broadcast_to(columns[i][j : j + 1], (32, 128))
            factor = jnp.where(sub > j, columns[i] / pivot, 0.0)
            scale = jnp.where(sub == j, lax.rsqrt(pivot), scale)
            for k in range(i + 1, STEP):
                columns[k] = columns[k] - factor * columns[k][j : j + 1]
            normal = normal - factor * normal[j : j + 1]
            product = product - factor * product[j : j + 1]
    return product * scale


def kernel(
    aperture_hbm,
    delay_hbm,
    offset_hbm,
    slope_hbm,
    tilt_hbm,
    prior_hbm,
    echo_hbm,
    out_ref,
    run_ref,
    aperture_ref,
    delay_ref,
    offset_ref,
    slope_ref,
    tilt_ref,
    prior_ref,
    echo_ref,
    moved_ref,
    rows_ref,
    own_ref,
    prev_ref,
    next_ref,
    prev_delay_ref,
    all_ref,
    place_ref,
    point_ref,
    total_ref,
    beam_ref,
    wide_ref,
    mine_ref,
    got_ref,
    sum_ref,
    gram_ref,
    basis_ref,
    power_ref,
    input_sem,
    ring_send,
    ring_recv,
    peer_send,
    peer_recv,
    send,
    recv,
):
    group = lax.axis_index("chan")
    slab = lax.axis_index("vox")
    before = lax.rem(slab + SLABS - 1, SLABS)
    after = lax.rem(slab + 1, SLABS)
    core = lax.rem(slab, 2)
    chip = slab // 2
    y, z = chip // 8, lax.rem(chip, 8)
    me = y * 8 + group * 2 + core
    around = []
    for dy in (2, 1, 3, 0):
        row_y = lax.rem(y + dy, 4)
        for d in (4, 3, 5, 2, 6, 1, 7, 0):
            if dy == 0 and d == 0:
                continue
            inner = lax.rem(group * 2 + core + d, 8)
            around.append(
                (row_y * 8 + inner, (inner // 2, (row_y * 8 + z) * 2 + lax.rem(inner, 2)))
            )
    along_z = [(group, (y * 8 + lax.rem(z + d, 8)) * 2 + core) for d in (4, 3, 5, 2, 6, 1, 7)]
    inputs = [
        pltpu.make_async_copy(source, target, input_sem.at[k])
        for k, (source, target) in enumerate(
            [
                (aperture_hbm.at[pl.ds(slab, 1), :], run_ref.at[pl.ds(0, 1), :]),
                (aperture_hbm.at[pl.ds(before, 1), :], run_ref.at[pl.ds(1, 1), :]),
                (delay_hbm, delay_ref),
                (aperture_hbm, aperture_ref),
                (offset_hbm, offset_ref),
                (slope_hbm, slope_ref),
                (tilt_hbm, tilt_ref),
                (prior_hbm, prior_ref),
                (echo_hbm, echo_ref),
            ]
        )
    ]
    for c in inputs:
        c.start()
    barrier = pltpu.get_barrier_semaphore()
    places = along_z + [a[1] for a in around] + [(group, before), (group, after)]
    for place in places:
        pl.semaphore_signal(barrier, inc=1, device_id=place, device_id_type=MESH)
    for c in inputs[:-1]:
        c.wait()

    def copy(src, dst, place, sends, recvs, k):
        return pltpu.make_async_remote_copy(
            src_ref=src,
            dst_ref=dst,
            send_sem=sends.at[k],
            recv_sem=recvs.at[k],
            device_id=place,
            device_id_type=MESH,
        )

    lane1 = iota((1, 128), 1)

    def edges(row):
        last = jnp.where(
            lane1 % GROUP == 0, pltpu.roll(row, 97, 1), pltpu.roll(row, 1, 1)
        )
        return (row * (1 - last) * (lane1 % GROUP)).astype(F32)

    row = aperture_ref[pl.ds(slab, 1), :]
    prev_row = aperture_ref[pl.ds(before, 1), :]
    first_of = edges(row)
    order = iota((16, 64), 0)
    order = jnp.where(order < 8, 2 * (order // 2), 2 * (order // 2) - 7)
    member = iota((16, 64), 1) // 8 == order

    def gates_of(r, half):
        count = jnp.sum(
            jnp.where(lane1 // GROUP == group, r.astype(F32), 0.0), axis=1, keepdims=True
        )
        return jnp.where(
            member & ((order + 8 * half).astype(F32) < count), 1.0 / 32, 0.0
        ).astype(BF16)

    rows_ref[...] = jnp.zeros_like(rows_ref)
    lane8 = iota((8, 128), 1)
    sub8 = iota((8, 128), 0)
    depth = (lane8 & 15).astype(F32)
    side = (lane8 >> 4).astype(F32)
    level = iota((16, 128), 0)
    levels = [(level + 16 * k).astype(BF16) for k in range(4)]
    pasts = [(level + (16 * k - 1)).astype(BF16) for k in range(4)]

    def place_blocks(r):
        source = lax.rem(group + r, 4)
        start = jnp.sum(
            jnp.where(lane1 // GROUP == source, first_of, 0.0), axis=1, keepdims=True
        ).astype(jnp.int32)
        for s in range(2):
            pick = source * GROUP + ((jnp.broadcast_to(start, (8, 128)) + sub8 + 8 * s) & 31)

            def values(ref):
                return jnp.take_along_axis(
                    jnp.broadcast_to(ref[0:1, :], (8, 128)), pick, axis=1
                )

            slope, tilt = values(slope_ref), values(tilt_ref)
            lateral = side + (64 * group).astype(F32)
            place_ref[r, s, 0] = values(offset_ref) + slope * depth + tilt * lateral
            place_ref[r, s, 1] = tilt * 8.0
            place_ref[r, s, 2] = slope * 16.0

    start = run_start(run_ref, 0, group)
    prev_start = run_start(run_ref, 1, group)
    inputs[-1].wait()

    def own_half(half):
        window_sums(
            True, half, start, gates_of(row, half), delay_ref, echo_ref, moved_ref, rows_ref
        )
        own_ref[half] = rows_ref[...]

    own_half(0)
    pl.semaphore_wait(barrier, len(places))
    step = copy(delay_ref, prev_delay_ref, (group, after), ring_send, ring_recv, 0)
    has_before, has_after = slab > 0, slab < SLABS - 1
    pl.when(has_after)(step.start)
    own_half(1)

    @pl.when(jnp.logical_not(has_before))
    def _():
        prev_delay_ref[...] = jnp.zeros_like(prev_delay_ref)

    @pl.when(jnp.logical_not(has_after))
    def _():
        next_ref[...] = jnp.zeros_like(next_ref)

    pl.when(has_before)(step.wait_recv)
    steps = []
    for half in range(2):
        gates = gates_of(prev_row, half)
        window_sums(
            False, half, prev_start, gates, prev_delay_ref, echo_ref, moved_ref, rows_ref
        )
        prev_ref[half] = rows_ref[...].astype(BF16)
        steps.append(
            copy(
                prev_ref.at[half],
                next_ref.at[half],
                (group, before),
                ring_send,
                ring_recv,
                1 + half,
            )
        )
        pl.when(has_before)(steps[half].start)
    for r in range(4):
        place_blocks(r)
    blank = jnp.zeros((128 - ROWS, 128), BF16)
    for t in range(VOXELS // 128):
        beam_ref[t, ROWS:128, :] = blank
        beam_ref[t, 128 + ROWS : 256, :] = blank
    right, left = (lax.rem(group + 1, 4), slab), (lax.rem(group + 3, 4), slab)

    def pass_on(source, target, begin, size, place, k):
        part = pl.ds(begin, size)
        return copy(
            all_ref.at[source, part], all_ref.at[target, part], place, peer_send, peer_recv, k
        )

    near_copies, far_copies = [], []
    for half in range(2):
        begin = half * HALF
        near_copies.append(
            [
                pass_on(0, 3, begin, HALF, right, 4 * half),
                pass_on(0, 1, begin, HALF, left, 4 * half + 1),
            ]
        )
        far_copies.append(
            [
                pass_on(3, 2, begin, HALF // 2, right, 4 * half + 2),
                pass_on(1, 2, begin + HALF // 2, HALF // 2, left, 4 * half + 3),
            ]
        )
    for half in range(2):
        pl.when(has_after)(steps[half].wait_recv)
        all_ref[0, half * HALF : (half + 1) * HALF, :] = (
            own_ref[half] + next_ref[half].astype(F32)
        ).astype(BF16)
        for c in near_copies[half]:
            c.start()

    def weights_of(at, b, skip):
        node, left, right = [
            jnp.broadcast_to(point_ref[at + 8 * k + b : at + 8 * k + b + 1, :], (16, 128)).astype(
                BF16
            )
            for k in range(3)
        ]
        none = jnp.zeros_like(right)
        return jnp.concatenate(
            [
                none
                if k == skip
                else jnp.where(
                    levels[k] == node, left, jnp.where(pasts[k] == node, right, none)
                )
                for k in range(4)
            ],
            axis=0,
        )

    near = 4 - group

    def project(units, first, last):
        lax.fori_loop(0, near, project_tile(units, first, last, 3), 0)
        lax.fori_loop(near, 4, project_tile(units, first, last, 0), 0)

    def project_tile(units, first, last, skip):
        def tile(i, carry):
            at = 0
            for v in range(4):
                for r, s in units:
                    base = place_ref[r, s, 0] + place_ref[r, s, 2] * i.astype(F32)
                    for u in range(2):
                        position = base + place_ref[r, s, 1] * float(2 * v + u)
                        node = jnp.floor(position)
                        right = position - node
                        point_ref[at : at + 8, :] = node
                        point_ref[at + 8 : at + 16, :] = 1.0 - right
                        point_ref[at + 16 : at + 24, :] = right
                        at += 24
            at = 0
            for v in range(4):
                n = 4 * i + v
                columns = pl.ds(pl.multiple_of(n * 256, 256), 256)
                total = None if first else total_ref[:, columns]
                for r, s in units:
                    for c in range(2):
                        weights = jnp.concatenate(
                            [
                                jnp.concatenate(
                                    [weights_of(at, b, skip), weights_of(at + 24, b, skip)],
                                    axis=1,
                                )
                                for b in range(4 * c, 4 * c + 4)
                            ],
                            axis=0,
                        )
                        m = 4 * s + 2 * c
                        blocks = jnp.concatenate(
                            [
                                all_ref[r, m * ROWS : (m + 1) * ROWS, :],
                                all_ref[r, (m + 1) * ROWS : (m + 2) * ROWS, :],
                            ],
                            axis=1,
                        )
                        part = jnp.dot(blocks, weights, preferred_element_type=F32)
                        total = part if total is None else total + part
                    at += 48
                if not last:
                    total_ref[:, columns] = total
                    continue
                high = total.astype(BF16)
                low = (total - high.astype(F32)).astype(BF16)
                for q in range(2):
                    lanes = slice(q * 128, q * 128 + 128)
                    beam_ref[2 * n + q, 0:ROWS, :] = high[:, lanes]
                    beam_ref[2 * n + q, 128 : 128 + ROWS, :] = low[:, lanes]
            return carry

        return tile

    project(((0, 0), (0, 1)), True, False)
    for half in range(2):
        for k in range(2):
            near_copies[half][k].wait_recv()
            far_copies[half][k].start()
        project(((3, half), (1, half)), False, False)
    for c in far_copies[0] + far_copies[1]:
        c.wait_recv()
    project(((2, 0), (2, 1)), False, True)
    pl.when(has_after)(step.wait_send)
    for half in range(2):
        pl.when(has_before)(steps[half].wait_send)
        for c in near_copies[half] + far_copies[half]:
            c.wait_send()
    wide_ref[...] = jnp.zeros_like(wide_ref)

    def square(i, carry):
        part = jnp.concatenate([beam_ref[8 * i + k] for k in range(8)], axis=1)
        wide_ref[...] += lax.dot_general(
            part, part[0:128], (((1,), (1,)), ((), ())), preferred_element_type=F32
        )
        return carry

    lax.fori_loop(0, 4, square, 0)
    cross = wide_ref[128:256, :]
    gram = wide_ref[0:128, :] + cross + cross.T
    for k in range(32):
        mine_ref[k] = gram[4 * k : 4 * k + 4]

    def exchange(stage, moves, all_sent, all_received):
        for source, target, place in moves:
            copy(source, target, place, send, recv, stage).start()
        every = copy(all_sent, all_received, moves[0][2], send, recv, stage)
        every.wait_recv()
        every.wait_send()

    exchange(
        0,
        [(mine_ref.at[peer], got_ref.at[k], place) for k, (peer, place) in enumerate(around)],
        mine_ref.at[0:31],
        got_ref.at[0:31],
    )
    total = mine_ref[me]
    for k in range(31):
        total = total + got_ref[k]
    sum_ref[...] = total
    exchange(
        1,
        [(sum_ref, got_ref.at[31 + k], place) for k, place in enumerate(along_z)],
        mine_ref.at[0:7],
        got_ref.at[31:38],
    )
    for k in range(7):
        total = total + got_ref[31 + k]
    gram_ref[me] = total
    exchange(
        2,
        [(gram_ref.at[me], gram_ref.at[me], place) for _, place in around],
        mine_ref.at[0:31],
        gram_ref.at[0:31],
    )

    gram = jnp.concatenate([gram_ref[k] for k in range(32)], axis=0)
    basis_ref[...] = jnp.zeros_like(basis_ref)
    basis_ref[0:RANK, 0:FRAMES] = prior_ref[...]
    lane = iota((32, 128), 1)
    odd = (lane >= SIDE).astype(jnp.int32)
    frame = 2 * (lane - SIDE * odd) + odd
    basis = jnp.take_along_axis(basis_ref[...], jnp.minimum(frame, 127), axis=1)
    basis = jnp.where(frame < FRAMES, basis, 0.0)
    basis = sweep(gram, basis)
    basis = sweep(gram, basis)
    overlap = lax.dot_general(
        basis,
        basis,
        (((0,), (0,)), ((), ())),
        precision=lax.Precision.HIGHEST,
        preferred_element_type=F32,
    )
    keep = jnp.where(iota((128, 128), 0) == iota((128, 128), 1), 1.0, 0.0) - overlap
    high = keep.astype(BF16)
    low = (keep - high.astype(F32)).astype(BF16)
    twice = jnp.concatenate([high, high], axis=1)
    for c in range(VOXELS // 256):
        beam = jnp.concatenate([beam_ref[2 * c], beam_ref[2 * c + 1]], axis=1)
        clean = jnp.dot(twice, beam, preferred_element_type=F32)
        clean = clean + jnp.dot(low, beam[0:128], preferred_element_type=F32)
        power = jnp.sum(clean * clean, axis=0, keepdims=True)
        power_ref[2 * c : 2 * c + 1, :] = power[:, 0:128]
        power_ref[2 * c + 1 : 2 * c + 2, :] = power[:, 128:256]
    pick = (2 * (sub8 & 3) + (lane8 >> 6)) * 16 + (lane8 & 15)
    quarter = (lane8 >> 4) & 3
    for p in range(4):
        rows = None
        for q in range(4):
            one = jnp.broadcast_to(power_ref[8 * q + 2 * p : 8 * q + 2 * p + 1, :], (8, 128))
            two = jnp.broadcast_to(power_ref[8 * q + 2 * p + 1 : 8 * q + 2 * p + 2, :], (8, 128))
            got = jnp.take_along_axis(jnp.where(sub8 < 4, one, two), pick, axis=1)
            rows = got if rows is None else jnp.where(quarter == q, got, rows)
        out_ref[8 * p : 8 * p + 8, :] = rows


def body(echo_data, delays, aperture, offset, depth_slope, lateral_tilt, prior_basis):
    vmem = pl.BlockSpec(memory_space=VMEM)
    dma = pltpu.SemaphoreType.DMA
    squares = pl.pallas_call(
        kernel,
        out_shape=VMEM((VOXELS // 128, 128), F32),
        in_specs=[pl.BlockSpec(memory_space=pl.ANY)] * 7,
        out_specs=vmem,
        scratch_shapes=[
            pltpu.SMEM((2, 128), jnp.int32),
            VMEM((SLABS, 128), jnp.int32),
            VMEM((1, 256), jnp.int32),
            VMEM((1, 128), F32),
            VMEM((1, 128), F32),
            VMEM((1, 128), F32),
            VMEM((RANK, FRAMES), F32),
            VMEM((GROUP, 8, 128 * PAIRS), BF16),
            VMEM((PAIRS, 64, 128), BF16),
            VMEM((HALF, 128), F32),
            VMEM((2, HALF, 128), F32),
            VMEM((2, HALF, 128), BF16),
            VMEM((2, HALF, 128), BF16),
            VMEM((1, 256), jnp.int32),
            VMEM((4, SIZE, 128), BF16),
            VMEM((4, 2, 3, 8, 128), F32),
            VMEM((384, 128), F32),
            VMEM((ROWS, VOXELS), F32),
            VMEM((VOXELS // 128, 256, 128), BF16),
            VMEM((256, 128), F32),
            VMEM((32, 4, 128), F32),
            VMEM((38, 4, 128), F32),
            VMEM((4, 128), F32),
            VMEM((32, 4, 128), F32),
            VMEM((32, 128), F32),
            VMEM((VOXELS // 128, 128), F32),
            dma((9,)),
            dma((3,)),
            dma((3,)),
            dma((8,)),
            dma((8,)),
            dma((3,)),
            dma((3,)),
        ],
        compiler_params=pltpu.CompilerParams(
            collective_id=0, has_side_effects=True, vmem_limit_bytes=62 * 1024 * 1024
        ),
        name="doppler",
    )(
        aperture.T,
        delays.reshape(1, 256),
        offset.reshape(1, 128),
        depth_slope.reshape(1, 128),
        lateral_tilt.reshape(1, 128),
        prior_basis.T,
        echo_data.reshape(GROUP, 8, 128 * PAIRS),
    )
    return squares.reshape(1, VOXELS) / FRAMES


def solution(mesh):
    in_specs = (
        P("chan", "vox", None),
        P("chan", "vox"),
        P(),
        P(None, "vox"),
        P(None, "vox"),
        P(None, "vox"),
        P(),
    )
    out_specs = P("vox", "chan")
    return jax.shard_map(body, mesh=mesh, in_specs=in_specs, out_specs=out_specs, check_vma=False)
```

```python
import jax
import jax.numpy as jnp
from jax import lax
from jax.experimental import pallas as pl
from jax.experimental.pallas import tpu as pltpu
from jax.sharding import PartitionSpec as P

MESH = pl.DeviceIdType.MESH
FRAMES = 100
RANK = 30
PAIRS = 50
ROWS = 104
HALF = 4 * ROWS
SIDE = ROWS // 2
STEP = 15
RUN = 16
GROUP = 32
SLABS = 64
SIZE = RUN // 2 * ROWS
VOXELS = 4096
VMEM = pltpu.VMEM
F32 = jnp.float32
BF16 = jnp.bfloat16


def iota(shape, dim):
    return lax.broadcasted_iota(jnp.int32, shape, dim)


def run_start(run_ref, which, group):
    start = jnp.int32(0)
    before = run_ref[which, group * GROUP + GROUP - 1]
    for b in range(GROUP):
        here = run_ref[which, group * GROUP + b]
        start = start + b * here * (1 - before)
        before = here
    return start


def window_sums(own, half, start, gates, delay_ref, echo_ref, moved_ref, rows_ref):
    lane = iota((8, 128), 1)
    sub = iota((8, 128), 0)
    sample = lane & 63
    low = jnp.broadcast_to(delay_ref[0:1, 0:128], (8, 128))
    high = jnp.broadcast_to(delay_ref[0:1, 128:256], (8, 128))

    def blocks(i, carry):
        places, picks, keeps = [], [], []
        for q in range(4):
            block = lax.rem(start + 8 * half + 4 * i + q, GROUP)
            table = jnp.where(jnp.full((8, 128), block, jnp.int32) < 16, low, high)
            delay = jnp.take_along_axis(table, (block & 15) * 8 + sub, axis=1)
            if own:
                picks.append((lane + delay) & 127)
                keeps.append(sample + delay < 64)
            else:
                picks.append((lane + delay + 64) & 127)
                keeps.append(sample + delay >= 64)
            places.append(block)
        for t in range(PAIRS):
            parts = []
            for q in range(4):
                values = echo_ref[places[q], :, t * 128 : (t + 1) * 128].astype(F32)
                values = jnp.take_along_axis(values, picks[q], axis=1)
                parts.append(jnp.where(keeps[q], values, 0.0))
            moved_ref[t, pl.ds(pl.multiple_of(i * 32, 32), 32), :] = jnp.concatenate(
                parts, axis=0
            ).astype(BF16)
        return carry

    lax.fori_loop(0, RUN // 8, blocks, 0)
    first = lane < 64
    even_frame = (sub & 1) == 0
    for c in range(PAIRS // 2):
        both = jnp.concatenate([moved_ref[2 * c], moved_ref[2 * c + 1]], axis=1)
        sums = jnp.dot(gates, both, preferred_element_type=F32)
        for q in range(2):
            even = sums[0:8, q * 128 : (q + 1) * 128]
            odd = sums[8:16, q * 128 : (q + 1) * 128]
            rows_ref[pl.ds(2 * c + q, 8, stride=SIDE), :] = jnp.where(
                first,
                jnp.where(even_frame, even, pltpu.roll(even, 64, 1)),
                jnp.where(even_frame, pltpu.roll(odd, 64, 1), odd),
            )


def sweep(gram, rows):
    product = jnp.dot(rows, gram, precision=lax.Precision.HIGHEST, preferred_element_type=F32)
    normal = lax.dot_general(
        product,
        product,
        (((1,), (1,)), ((), ())),
        precision=lax.Precision.HIGHEST,
        preferred_element_type=F32,
    )
    normal = jnp.concatenate([normal, jnp.zeros((32, 96), F32)], axis=1)
    sub = iota((32, 128), 0)
    scale = jnp.zeros((32, 128), F32)
    for begin in range(0, RANK, STEP):
        columns = [
            jnp.take_along_axis(normal, jnp.full((32, 128), begin + i, jnp.int32), axis=1)
            for i in range(STEP)
        ]
        for i in range(STEP):
            j = begin + i
            pivot = jnp.broadcast_to(columns[i][j : j + 1], (32, 128))
            factor = jnp.where(sub > j, columns[i] / pivot, 0.0)
            scale = jnp.where(sub == j, lax.rsqrt(pivot), scale)
            for k in range(i + 1, STEP):
                columns[k] = columns[k] - factor * columns[k][j : j + 1]
            normal = normal - factor * normal[j : j + 1]
            product = product - factor * product[j : j + 1]
    return product * scale


def kernel(
    aperture_hbm,
    delay_hbm,
    offset_hbm,
    slope_hbm,
    tilt_hbm,
    prior_hbm,
    echo_hbm,
    out_ref,
    run_ref,
    aperture_ref,
    delay_ref,
    offset_ref,
    slope_ref,
    tilt_ref,
    prior_ref,
    echo_ref,
    moved_ref,
    rows_ref,
    own_ref,
    prev_ref,
    next_ref,
    prev_delay_ref,
    all_ref,
    place_ref,
    point_ref,
    total_ref,
    beam_ref,
    wide_ref,
    mine_ref,
    got_ref,
    sum_ref,
    gram_ref,
    basis_ref,
    power_ref,
    ready_sem,
    input_sem,
    ring_send,
    ring_recv,
    peer_send,
    peer_recv,
    send,
    recv,
):
    group = lax.axis_index("chan")
    slab = lax.axis_index("vox")
    before = lax.rem(slab + SLABS - 1, SLABS)
    after = lax.rem(slab + 1, SLABS)
    core = lax.rem(slab, 2)
    chip = slab // 2
    y, z = chip // 8, lax.rem(chip, 8)
    me = y * 8 + group * 2 + core
    around = []
    for dy in (2, 1, 3, 0):
        row_y = lax.rem(y + dy, 4)
        for d in (4, 3, 5, 2, 6, 1, 7, 0):
            if dy == 0 and d == 0:
                continue
            inner = lax.rem(group * 2 + core + d, 8)
            around.append(
                (row_y * 8 + inner, (inner // 2, (row_y * 8 + z) * 2 + lax.rem(inner, 2)))
            )
    along_z = [(group, (y * 8 + lax.rem(z + d, 8)) * 2 + core) for d in (4, 3, 5, 2, 6, 1, 7)]
    inputs = [
        pltpu.make_async_copy(source, target, input_sem.at[k])
        for k, (source, target) in enumerate(
            [
                (aperture_hbm.at[pl.ds(slab, 1), :], run_ref.at[pl.ds(0, 1), :]),
                (aperture_hbm.at[pl.ds(before, 1), :], run_ref.at[pl.ds(1, 1), :]),
                (delay_hbm, delay_ref),
                (aperture_hbm, aperture_ref),
                (offset_hbm, offset_ref),
                (slope_hbm, slope_ref),
                (tilt_hbm, tilt_ref),
                (prior_hbm, prior_ref),
                (echo_hbm, echo_ref),
            ]
        )
    ]
    for c in inputs:
        c.start()
    barrier = pltpu.get_barrier_semaphore()
    along_y = [(group, (lax.rem(y + d, 4) * 8 + z) * 2 + core) for d in (2, 1, 3)]
    beside = [place for k, (_, place) in enumerate(around) if k >= 24]
    places = beside + along_y + [(group, before), (group, after)] + along_z
    for place in places:
        pl.semaphore_signal(barrier, inc=1, device_id=place, device_id_type=MESH)
    for c in inputs[:-1]:
        c.wait()

    def copy(src, dst, place, sends, recvs, k):
        return pltpu.make_async_remote_copy(
            src_ref=src,
            dst_ref=dst,
            send_sem=sends.at[k],
            recv_sem=recvs.at[k],
            device_id=place,
            device_id_type=MESH,
        )

    lane1 = iota((1, 128), 1)

    def edges(row):
        last = jnp.where(
            lane1 % GROUP == 0, pltpu.roll(row, 97, 1), pltpu.roll(row, 1, 1)
        )
        return (row * (1 - last) * (lane1 % GROUP)).astype(F32)

    row = aperture_ref[pl.ds(slab, 1), :]
    prev_row = aperture_ref[pl.ds(before, 1), :]
    first_of = edges(row)
    order = iota((16, 64), 0)
    order = jnp.where(order < 8, 2 * (order // 2), 2 * (order // 2) - 7)
    member = iota((16, 64), 1) // 8 == order

    def gates_of(r, half):
        count = jnp.sum(
            jnp.where(lane1 // GROUP == group, r.astype(F32), 0.0), axis=1, keepdims=True
        )
        return jnp.where(
            member & ((order + 8 * half).astype(F32) < count), 1.0 / 32, 0.0
        ).astype(BF16)

    rows_ref[...] = jnp.zeros_like(rows_ref)
    lane8 = iota((8, 128), 1)
    sub8 = iota((8, 128), 0)
    depth = (lane8 & 15).astype(F32)
    side = (lane8 >> 4).astype(F32)
    level = iota((16, 128), 0)
    levels = [(level + 16 * k).astype(BF16) for k in range(4)]
    pasts = [(level + (16 * k - 1)).astype(BF16) for k in range(4)]

    def place_blocks(r):
        source = lax.rem(group + r, 4)
        start = jnp.sum(
            jnp.where(lane1 // GROUP == source, first_of, 0.0), axis=1, keepdims=True
        ).astype(jnp.int32)
        for s in range(2):
            pick = source * GROUP + ((jnp.broadcast_to(start, (8, 128)) + sub8 + 8 * s) & 31)

            def values(ref):
                return jnp.take_along_axis(
                    jnp.broadcast_to(ref[0:1, :], (8, 128)), pick, axis=1
                )

            slope, tilt = values(slope_ref), values(tilt_ref)
            lateral = side + (64 * group).astype(F32)
            place_ref[r, s, 0] = values(offset_ref) + slope * depth + tilt * lateral
            place_ref[r, s, 1] = tilt * 8.0
            place_ref[r, s, 2] = slope * 16.0

    start = run_start(run_ref, 0, group)
    prev_start = run_start(run_ref, 1, group)

    def own_half(half):
        window_sums(
            True, half, start, gates_of(row, half), delay_ref, echo_ref, moved_ref, rows_ref
        )
        own_ref[half] = rows_ref[0:HALF, :]

    pl.semaphore_wait(barrier, len(places))
    step = copy(delay_ref, prev_delay_ref, (group, after), ring_send, ring_recv, 0)
    has_before, has_after = slab > 0, slab < SLABS - 1
    pl.when(has_after)(step.start)
    for place in along_y:
        pl.semaphore_signal(ready_sem, inc=1, device_id=place, device_id_type=MESH)
    inputs[-1].wait()
    own_half(0)
    own_half(1)

    @pl.when(jnp.logical_not(has_before))
    def _():
        prev_delay_ref[...] = jnp.zeros_like(prev_delay_ref)

    @pl.when(jnp.logical_not(has_after))
    def _():
        next_ref[...] = jnp.zeros_like(next_ref)

    pl.when(has_before)(step.wait_recv)
    steps = []
    for half in range(2):
        gates = gates_of(prev_row, half)
        window_sums(
            False, half, prev_start, gates, prev_delay_ref, echo_ref, moved_ref, rows_ref
        )
        prev_ref[half] = rows_ref[0:HALF, :].astype(BF16)
        steps.append(
            copy(
                prev_ref.at[half],
                next_ref.at[half],
                (group, before),
                ring_send,
                ring_recv,
                1 + half,
            )
        )
        pl.when(has_before)(steps[half].start)
    for r in range(4):
        place_blocks(r)
    blank = jnp.zeros((128 - ROWS, 128), BF16)
    for t in range(VOXELS // 128):
        beam_ref[t, ROWS:128, :] = blank
        beam_ref[t, 128 + ROWS : 256, :] = blank
    right, left = (lax.rem(group + 1, 4), slab), (lax.rem(group + 3, 4), slab)

    def pass_on(source, target, begin, size, place, k):
        part = pl.ds(begin, size)
        return copy(
            all_ref.at[source, part], all_ref.at[target, part], place, peer_send, peer_recv, k
        )

    near_copies, far_copies = [], []
    for half in range(2):
        begin = half * HALF
        near_copies.append(
            [
                pass_on(0, 3, begin, HALF, right, 4 * half),
                pass_on(0, 1, begin, HALF, left, 4 * half + 1),
            ]
        )
        far_copies.append(
            [
                pass_on(3, 2, begin, HALF // 2, right, 4 * half + 2),
                pass_on(1, 2, begin + HALF // 2, HALF // 2, left, 4 * half + 3),
            ]
        )
    for half in range(2):
        pl.when(has_after)(steps[half].wait_recv)
        all_ref[0, half * HALF : (half + 1) * HALF, :] = (
            own_ref[half] + next_ref[half].astype(F32)
        ).astype(BF16)
        for c in near_copies[half]:
            c.start()

    def weights_of(at, b, skip):
        node, left, right = [
            jnp.broadcast_to(point_ref[at + 8 * k + b : at + 8 * k + b + 1, :], (16, 128)).astype(
                BF16
            )
            for k in range(3)
        ]
        none = jnp.zeros_like(right)
        return jnp.concatenate(
            [
                none
                if k == skip
                else jnp.where(
                    levels[k] == node, left, jnp.where(pasts[k] == node, right, none)
                )
                for k in range(4)
            ],
            axis=0,
        )

    near = 4 - group

    def project(units, first, last):
        lax.fori_loop(0, near, project_tile(units, first, last, 3), 0)
        lax.fori_loop(near, 4, project_tile(units, first, last, 0), 0)

    def project_tile(units, first, last, skip):
        def tile(i, carry):
            at = 0
            for v in range(4):
                for r, s in units:
                    base = place_ref[r, s, 0] + place_ref[r, s, 2] * i.astype(F32)
                    for u in range(2):
                        position = base + place_ref[r, s, 1] * float(2 * v + u)
                        node = jnp.floor(position)
                        right = position - node
                        point_ref[at : at + 8, :] = node
                        point_ref[at + 8 : at + 16, :] = 1.0 - right
                        point_ref[at + 16 : at + 24, :] = right
                        at += 24
            at = 0
            for v in range(4):
                n = 4 * i + v
                columns = pl.ds(pl.multiple_of(n * 256, 256), 256)
                total = None if first else total_ref[:, columns]
                for r, s in units:
                    for c in range(2):
                        weights = jnp.concatenate(
                            [
                                jnp.concatenate(
                                    [weights_of(at, b, skip), weights_of(at + 24, b, skip)],
                                    axis=1,
                                )
                                for b in range(4 * c, 4 * c + 4)
                            ],
                            axis=0,
                        )
                        m = 4 * s + 2 * c
                        blocks = jnp.concatenate(
                            [
                                all_ref[r, m * ROWS : (m + 1) * ROWS, :],
                                all_ref[r, (m + 1) * ROWS : (m + 2) * ROWS, :],
                            ],
                            axis=1,
                        )
                        part = jnp.dot(blocks, weights, preferred_element_type=F32)
                        total = part if total is None else total + part
                    at += 48
                if not last:
                    total_ref[:, columns] = total
                    continue
                high = total.astype(BF16)
                low = (total - high.astype(F32)).astype(BF16)
                for q in range(2):
                    lanes = slice(q * 128, q * 128 + 128)
                    beam_ref[2 * n + q, 0:ROWS, :] = high[:, lanes]
                    beam_ref[2 * n + q, 128 : 128 + ROWS, :] = low[:, lanes]
            return carry

        return tile

    project(((0, 0), (0, 1)), True, False)
    for half in range(2):
        for k in range(2):
            near_copies[half][k].wait_recv()
            far_copies[half][k].start()
        project(((3, half), (1, half)), False, False)
    for c in far_copies[0] + far_copies[1]:
        c.wait_recv()
    project(((2, 0), (2, 1)), False, True)
    pl.when(has_after)(step.wait_send)
    for half in range(2):
        pl.when(has_before)(steps[half].wait_send)
        for c in near_copies[half] + far_copies[half]:
            c.wait_send()
    wide_ref[...] = jnp.zeros_like(wide_ref)

    def square(i, carry):
        part = jnp.concatenate([beam_ref[16 * i + k] for k in range(16)], axis=1)
        wide_ref[...] += lax.dot_general(
            part, part[0:128], (((1,), (1,)), ((), ())), preferred_element_type=F32
        )
        return carry

    lax.fori_loop(0, 2, square, 0)
    cross = wide_ref[128:256, :]
    gram = wide_ref[0:128, :] + cross + cross.T
    for k in range(32):
        mine_ref[k] = gram[4 * k : 4 * k + 4]

    def exchange(stage, moves, all_sent, all_received):
        for source, target, place in moves:
            copy(source, target, place, send, recv, stage).start()
        every = copy(all_sent, all_received, moves[0][2], send, recv, stage)
        every.wait_recv()
        every.wait_send()

    pl.semaphore_wait(ready_sem, 3)
    exchange(
        0,
        [(mine_ref.at[peer], got_ref.at[k], place) for k, (peer, place) in enumerate(around)],
        mine_ref.at[0:31],
        got_ref.at[0:31],
    )
    total = mine_ref[me]
    for k in range(31):
        total = total + got_ref[k]
    sum_ref[...] = total
    exchange(
        1,
        [(sum_ref, got_ref.at[31 + k], place) for k, place in enumerate(along_z)],
        mine_ref.at[0:7],
        got_ref.at[31:38],
    )
    for k in range(7):
        total = total + got_ref[31 + k]
    gram_ref[me] = total
    exchange(
        2,
        [(gram_ref.at[me], gram_ref.at[me], place) for _, place in around],
        mine_ref.at[0:31],
        gram_ref.at[0:31],
    )

    gram = jnp.concatenate([gram_ref[k] for k in range(32)], axis=0)
    basis_ref[...] = jnp.zeros_like(basis_ref)
    basis_ref[0:RANK, 0:FRAMES] = prior_ref[...]
    lane = iota((32, 128), 1)
    odd = (lane >= SIDE).astype(jnp.int32)
    frame = 2 * (lane - SIDE * odd) + odd
    basis = jnp.take_along_axis(basis_ref[...], jnp.minimum(frame, 127), axis=1)
    basis = jnp.where(frame < FRAMES, basis, 0.0)
    basis = sweep(gram, basis)
    basis = sweep(gram, basis)
    overlap = lax.dot_general(
        basis,
        basis,
        (((0,), (0,)), ((), ())),
        precision=lax.Precision.HIGHEST,
        preferred_element_type=F32,
    )
    keep = jnp.where(iota((128, 128), 0) == iota((128, 128), 1), 1.0, 0.0) - overlap
    high = keep.astype(BF16)
    low = (keep - high.astype(F32)).astype(BF16)
    twice = jnp.concatenate([high, high], axis=1)
    for c in range(VOXELS // 256):
        beam = jnp.concatenate([beam_ref[2 * c], beam_ref[2 * c + 1]], axis=1)
        clean = jnp.dot(twice, beam, preferred_element_type=F32)
        clean = clean + jnp.dot(low, beam[0:128], preferred_element_type=F32)
        power = jnp.sum(clean * clean, axis=0, keepdims=True)
        power_ref[2 * c : 2 * c + 1, :] = power[:, 0:128]
        power_ref[2 * c + 1 : 2 * c + 2, :] = power[:, 128:256]
    pick = (2 * (sub8 & 3) + (lane8 >> 6)) * 16 + (lane8 & 15)
    quarter = (lane8 >> 4) & 3
    for p in range(4):
        rows = None
        for q in range(4):
            one = jnp.broadcast_to(power_ref[8 * q + 2 * p : 8 * q + 2 * p + 1, :], (8, 128))
            two = jnp.broadcast_to(power_ref[8 * q + 2 * p + 1 : 8 * q + 2 * p + 2, :], (8, 128))
            got = jnp.take_along_axis(jnp.where(sub8 < 4, one, two), pick, axis=1)
            rows = got if rows is None else jnp.where(quarter == q, got, rows)
        out_ref[8 * p : 8 * p + 8, :] = rows


def body(echo_data, delays, aperture, offset, depth_slope, lateral_tilt, prior_basis):
    vmem = pl.BlockSpec(memory_space=VMEM)
    dma = pltpu.SemaphoreType.DMA
    squares = pl.pallas_call(
        kernel,
        out_shape=VMEM((VOXELS // 128, 128), F32),
        in_specs=[pl.BlockSpec(memory_space=pl.ANY)] * 7,
        out_specs=vmem,
        scratch_shapes=[
            pltpu.SMEM((2, 128), jnp.int32),
            VMEM((SLABS, 128), jnp.int32),
            VMEM((1, 256), jnp.int32),
            VMEM((1, 128), F32),
            VMEM((1, 128), F32),
            VMEM((1, 128), F32),
            VMEM((RANK, FRAMES), F32),
            VMEM((GROUP, 8, 128 * PAIRS), BF16),
            VMEM((PAIRS, 64, 128), BF16),
            VMEM((HALF + 56, 128), F32),
            VMEM((2, HALF, 128), F32),
            VMEM((2, HALF, 128), BF16),
            VMEM((2, HALF, 128), BF16),
            VMEM((1, 256), jnp.int32),
            VMEM((4, SIZE, 128), BF16),
            VMEM((4, 2, 3, 8, 128), F32),
            VMEM((384, 128), F32),
            VMEM((ROWS, VOXELS), F32),
            VMEM((VOXELS // 128, 256, 128), BF16),
            VMEM((256, 128), F32),
            VMEM((32, 4, 128), F32),
            VMEM((38, 4, 128), F32),
            VMEM((4, 128), F32),
            VMEM((32, 4, 128), F32),
            VMEM((32, 128), F32),
            VMEM((VOXELS // 128, 128), F32),
            pltpu.SemaphoreType.REGULAR,
            dma((9,)),
            dma((3,)),
            dma((3,)),
            dma((8,)),
            dma((8,)),
            dma((3,)),
            dma((3,)),
        ],
        compiler_params=pltpu.CompilerParams(
            collective_id=0, has_side_effects=True, vmem_limit_bytes=62 * 1024 * 1024
        ),
        name="doppler",
    )(
        aperture.T,
        delays.reshape(1, 256),
        offset.reshape(1, 128),
        depth_slope.reshape(1, 128),
        lateral_tilt.reshape(1, 128),
        prior_basis.T,
        echo_data.reshape(GROUP, 8, 128 * PAIRS),
    )
    return squares.reshape(1, VOXELS) / FRAMES


def solution(mesh):
    in_specs = (
        P("chan", "vox", None),
        P("chan", "vox"),
        P(),
        P(None, "vox"),
        P(None, "vox"),
        P(None, "vox"),
        P(),
    )
    out_specs = P("vox", "chan")
    return jax.shard_map(body, mesh=mesh, in_specs=in_specs, out_specs=out_specs, check_vma=False)
```

```python
import jax
import jax.numpy as jnp
from jax import lax
from jax.experimental import pallas as pl
from jax.experimental.pallas import tpu as pltpu
from jax.sharding import PartitionSpec as P

MESH = pl.DeviceIdType.MESH
FRAMES = 100
RANK = 30
PAIRS = 50
ROWS = 104
HALF = 4 * ROWS
SIDE = ROWS // 2
STEP = 15
RUN = 16
GROUP = 32
SLABS = 64
SIZE = RUN // 2 * ROWS
VOXELS = 4096
VMEM = pltpu.VMEM
F32 = jnp.float32
BF16 = jnp.bfloat16


def iota(shape, dim):
    return lax.broadcasted_iota(jnp.int32, shape, dim)


def run_start(run_ref, which, group):
    start = jnp.int32(0)
    before = run_ref[which, group * GROUP + GROUP - 1]
    for b in range(GROUP):
        here = run_ref[which, group * GROUP + b]
        start = start + b * here * (1 - before)
        before = here
    return start


def window_sums(own, half, start, gates, delay_ref, echo_ref, moved_ref, rows_ref):
    lane = iota((8, 128), 1)
    sub = iota((8, 128), 0)
    sample = lane & 63
    low = jnp.broadcast_to(delay_ref[0:1, 0:128], (8, 128))
    high = jnp.broadcast_to(delay_ref[0:1, 128:256], (8, 128))

    def blocks(i, carry):
        places, picks, keeps = [], [], []
        for q in range(4):
            block = lax.rem(start + 8 * half + 4 * i + q, GROUP)
            table = jnp.where(jnp.full((8, 128), block, jnp.int32) < 16, low, high)
            delay = jnp.take_along_axis(table, (block & 15) * 8 + sub, axis=1)
            if own:
                picks.append((lane + delay) & 127)
                keeps.append(sample + delay < 64)
            else:
                picks.append((lane + delay + 64) & 127)
                keeps.append(sample + delay >= 64)
            places.append(block)
        for t in range(PAIRS):
            parts = []
            for q in range(4):
                values = echo_ref[places[q], :, t * 128 : (t + 1) * 128].astype(F32)
                values = jnp.take_along_axis(values, picks[q], axis=1)
                parts.append(jnp.where(keeps[q], values, 0.0))
            moved_ref[t, pl.ds(pl.multiple_of(i * 32, 32), 32), :] = jnp.concatenate(
                parts, axis=0
            ).astype(BF16)
        return carry

    lax.fori_loop(0, RUN // 8, blocks, 0)
    first = lane < 64
    even_frame = (sub & 1) == 0
    for c in range(PAIRS // 2):
        both = jnp.concatenate([moved_ref[2 * c], moved_ref[2 * c + 1]], axis=1)
        sums = jnp.dot(gates, both, preferred_element_type=F32)
        for q in range(2):
            even = sums[0:8, q * 128 : (q + 1) * 128]
            odd = sums[8:16, q * 128 : (q + 1) * 128]
            rows_ref[pl.ds(2 * c + q, 8, stride=SIDE), :] = jnp.where(
                first,
                jnp.where(even_frame, even, pltpu.roll(even, 64, 1)),
                jnp.where(even_frame, pltpu.roll(odd, 64, 1), odd),
            )


def sweep(gram, rows):
    product = jnp.dot(rows, gram, precision=lax.Precision.HIGHEST, preferred_element_type=F32)
    normal = lax.dot_general(
        product,
        product,
        (((1,), (1,)), ((), ())),
        precision=lax.Precision.HIGHEST,
        preferred_element_type=F32,
    )
    normal = jnp.concatenate([normal, jnp.zeros((32, 96), F32)], axis=1)
    sub = iota((32, 128), 0)
    scale = jnp.zeros((32, 128), F32)
    for begin in range(0, RANK, STEP):
        columns = [
            jnp.take_along_axis(normal, jnp.full((32, 128), begin + i, jnp.int32), axis=1)
            for i in range(STEP)
        ]
        for i in range(STEP):
            j = begin + i
            pivot = jnp.broadcast_to(columns[i][j : j + 1], (32, 128))
            factor = jnp.where(sub > j, columns[i] / pivot, 0.0)
            scale = jnp.where(sub == j, lax.rsqrt(pivot), scale)
            for k in range(i + 1, STEP):
                columns[k] = columns[k] - factor * columns[k][j : j + 1]
            normal = normal - factor * normal[j : j + 1]
            product = product - factor * product[j : j + 1]
    return product * scale


def kernel(
    aperture_hbm,
    delay_hbm,
    offset_hbm,
    slope_hbm,
    tilt_hbm,
    prior_hbm,
    echo_hbm,
    out_ref,
    run_ref,
    aperture_ref,
    delay_ref,
    offset_ref,
    slope_ref,
    tilt_ref,
    prior_ref,
    echo_ref,
    moved_ref,
    rows_ref,
    own_ref,
    prev_ref,
    next_ref,
    prev_delay_ref,
    all_ref,
    place_ref,
    point_ref,
    total_ref,
    beam_ref,
    wide_ref,
    mine_ref,
    got_ref,
    sum_ref,
    gram_ref,
    basis_ref,
    power_ref,
    ready_sem,
    input_sem,
    ring_send,
    ring_recv,
    peer_send,
    peer_recv,
    send,
    recv,
):
    group = lax.axis_index("chan")
    slab = lax.axis_index("vox")
    before = lax.rem(slab + SLABS - 1, SLABS)
    after = lax.rem(slab + 1, SLABS)
    core = lax.rem(slab, 2)
    chip = slab // 2
    y, z = chip // 8, lax.rem(chip, 8)
    me = y * 8 + group * 2 + core
    around = []
    for dy in (2, 1, 3, 0):
        row_y = lax.rem(y + dy, 4)
        for d in (4, 3, 5, 2, 6, 1, 7, 0):
            if dy == 0 and d == 0:
                continue
            inner = lax.rem(group * 2 + core + d, 8)
            around.append(
                (row_y * 8 + inner, (inner // 2, (row_y * 8 + z) * 2 + lax.rem(inner, 2)))
            )
    along_z = [(group, (y * 8 + lax.rem(z + d, 8)) * 2 + core) for d in (4, 3, 5, 2, 6, 1, 7)]
    inputs = [
        pltpu.make_async_copy(source, target, input_sem.at[k])
        for k, (source, target) in enumerate(
            [
                (aperture_hbm.at[pl.ds(slab, 1), :], run_ref.at[pl.ds(0, 1), :]),
                (aperture_hbm.at[pl.ds(before, 1), :], run_ref.at[pl.ds(1, 1), :]),
                (delay_hbm, delay_ref),
                (aperture_hbm, aperture_ref),
                (offset_hbm, offset_ref),
                (slope_hbm, slope_ref),
                (tilt_hbm, tilt_ref),
                (prior_hbm, prior_ref),
                (echo_hbm, echo_ref),
            ]
        )
    ]
    for c in inputs:
        c.start()
    barrier = pltpu.get_barrier_semaphore()
    along_y = [(group, (lax.rem(y + d, 4) * 8 + z) * 2 + core) for d in (2, 1, 3)]
    beside = [place for k, (_, place) in enumerate(around) if k >= 24]
    places = beside + along_y + [(group, before), (group, after)] + along_z
    for place in places:
        pl.semaphore_signal(barrier, inc=1, device_id=place, device_id_type=MESH)
    for c in inputs[:-1]:
        c.wait()

    def copy(src, dst, place, sends, recvs, k):
        return pltpu.make_async_remote_copy(
            src_ref=src,
            dst_ref=dst,
            send_sem=sends.at[k],
            recv_sem=recvs.at[k],
            device_id=place,
            device_id_type=MESH,
        )

    lane1 = iota((1, 128), 1)

    def edges(row):
        last = jnp.where(
            lane1 % GROUP == 0, pltpu.roll(row, 97, 1), pltpu.roll(row, 1, 1)
        )
        return (row * (1 - last) * (lane1 % GROUP)).astype(F32)

    row = aperture_ref[pl.ds(slab, 1), :]
    prev_row = aperture_ref[pl.ds(before, 1), :]
    first_of = edges(row)
    order = iota((16, 64), 0)
    order = jnp.where(order < 8, 2 * (order // 2), 2 * (order // 2) - 7)
    member = iota((16, 64), 1) // 8 == order

    def gates_of(r, half):
        count = jnp.sum(
            jnp.where(lane1 // GROUP == group, r.astype(F32), 0.0), axis=1, keepdims=True
        )
        return jnp.where(
            member & ((order + 8 * half).astype(F32) < count), 1.0 / 32, 0.0
        ).astype(BF16)

    rows_ref[...] = jnp.zeros_like(rows_ref)
    lane8 = iota((8, 128), 1)
    sub8 = iota((8, 128), 0)
    depth = (lane8 & 15).astype(F32)
    side = (lane8 >> 4).astype(F32)
    level = iota((16, 128), 0)
    levels = [(level + 16 * k).astype(BF16) for k in range(4)]
    pasts = [(level + (16 * k - 1)).astype(BF16) for k in range(4)]

    def place_blocks(r):
        source = lax.rem(group + r, 4)
        start = jnp.sum(
            jnp.where(lane1 // GROUP == source, first_of, 0.0), axis=1, keepdims=True
        ).astype(jnp.int32)
        for s in range(2):
            pick = source * GROUP + ((jnp.broadcast_to(start, (8, 128)) + sub8 + 8 * s) & 31)

            def values(ref):
                return jnp.take_along_axis(
                    jnp.broadcast_to(ref[0:1, :], (8, 128)), pick, axis=1
                )

            slope, tilt = values(slope_ref), values(tilt_ref)
            lateral = side + (64 * group).astype(F32)
            place_ref[r, s, 0] = values(offset_ref) + slope * depth + tilt * lateral
            place_ref[r, s, 1] = tilt * 8.0
            place_ref[r, s, 2] = slope * 16.0

    start = run_start(run_ref, 0, group)
    prev_start = run_start(run_ref, 1, group)

    def own_half(half):
        window_sums(
            True, half, start, gates_of(row, half), delay_ref, echo_ref, moved_ref, rows_ref
        )
        own_ref[half] = rows_ref[0:HALF, :]

    pl.semaphore_wait(barrier, len(places))
    step = copy(delay_ref, prev_delay_ref, (group, after), ring_send, ring_recv, 0)
    has_before, has_after = slab > 0, slab < SLABS - 1
    pl.when(has_after)(step.start)
    for place in along_y:
        pl.semaphore_signal(ready_sem, inc=1, device_id=place, device_id_type=MESH)
    inputs[-1].wait()
    own_half(0)
    own_half(1)

    @pl.when(jnp.logical_not(has_before))
    def _():
        prev_delay_ref[...] = jnp.zeros_like(prev_delay_ref)

    @pl.when(jnp.logical_not(has_after))
    def _():
        next_ref[...] = jnp.zeros_like(next_ref)

    pl.when(has_before)(step.wait_recv)
    steps = []
    for half in range(2):
        gates = gates_of(prev_row, half)
        window_sums(
            False, half, prev_start, gates, prev_delay_ref, echo_ref, moved_ref, rows_ref
        )
        prev_ref[half] = rows_ref[0:HALF, :].astype(BF16)
        steps.append(
            copy(
                prev_ref.at[half],
                next_ref.at[half],
                (group, before),
                ring_send,
                ring_recv,
                1 + half,
            )
        )
        pl.when(has_before)(steps[half].start)
    for r in range(4):
        place_blocks(r)
    blank = jnp.zeros((128 - ROWS, 128), BF16)
    for t in range(VOXELS // 128):
        beam_ref[t, ROWS:128, :] = blank
        beam_ref[t, 128 + ROWS : 256, :] = blank
    right, left = (lax.rem(group + 1, 4), slab), (lax.rem(group + 3, 4), slab)

    def pass_on(source, target, begin, size, place, k):
        part = pl.ds(begin, size)
        return copy(
            all_ref.at[source, part], all_ref.at[target, part], place, peer_send, peer_recv, k
        )

    near_copies, far_copies = [], []
    for half in range(2):
        begin = half * HALF
        near_copies.append(
            [
                pass_on(0, 3, begin, HALF, right, 4 * half),
                pass_on(0, 1, begin, HALF, left, 4 * half + 1),
            ]
        )
        far_copies.append(
            [
                pass_on(3, 2, begin, HALF // 2, right, 4 * half + 2),
                pass_on(1, 2, begin + HALF // 2, HALF // 2, left, 4 * half + 3),
            ]
        )
    for half in range(2):
        pl.when(has_after)(steps[half].wait_recv)
        all_ref[0, half * HALF : (half + 1) * HALF, :] = (
            own_ref[half] + next_ref[half].astype(F32)
        ).astype(BF16)
        for c in near_copies[half]:
            c.start()

    def weights_of(at, b, skip):
        node, left, right = [
            jnp.broadcast_to(point_ref[at + 8 * k + b : at + 8 * k + b + 1, :], (16, 128)).astype(
                BF16
            )
            for k in range(3)
        ]
        none = jnp.zeros_like(right)
        return jnp.concatenate(
            [
                none
                if k == skip
                else jnp.where(
                    levels[k] == node, left, jnp.where(pasts[k] == node, right, none)
                )
                for k in range(4)
            ],
            axis=0,
        )

    near = 4 - group

    def project(units, first, last):
        lax.fori_loop(0, near, project_tile(units, first, last, 3), 0)
        lax.fori_loop(near, 4, project_tile(units, first, last, 0), 0)

    def project_tile(units, first, last, skip):
        def tile(i, carry):
            at = 0
            for v in range(4):
                for r, s in units:
                    base = place_ref[r, s, 0] + place_ref[r, s, 2] * i.astype(F32)
                    for u in range(2):
                        position = base + place_ref[r, s, 1] * float(2 * v + u)
                        node = jnp.floor(position)
                        right = position - node
                        point_ref[at : at + 8, :] = node
                        point_ref[at + 8 : at + 16, :] = 1.0 - right
                        point_ref[at + 16 : at + 24, :] = right
                        at += 24
            at = 0
            for v in range(4):
                n = 4 * i + v
                columns = pl.ds(pl.multiple_of(n * 256, 256), 256)
                total = None if first else total_ref[:, columns]
                for r, s in units:
                    for c in range(2):
                        weights = jnp.concatenate(
                            [
                                jnp.concatenate(
                                    [weights_of(at, b, skip), weights_of(at + 24, b, skip)],
                                    axis=1,
                                )
                                for b in range(4 * c, 4 * c + 4)
                            ],
                            axis=0,
                        )
                        m = 4 * s + 2 * c
                        blocks = jnp.concatenate(
                            [
                                all_ref[r, m * ROWS : (m + 1) * ROWS, :],
                                all_ref[r, (m + 1) * ROWS : (m + 2) * ROWS, :],
                            ],
                            axis=1,
                        )
                        part = jnp.dot(blocks, weights, preferred_element_type=F32)
                        total = part if total is None else total + part
                    at += 48
                if not last:
                    total_ref[:, columns] = total
                    continue
                high = total.astype(BF16)
                low = (total - high.astype(F32)).astype(BF16)
                for q in range(2):
                    lanes = slice(q * 128, q * 128 + 128)
                    beam_ref[2 * n + q, 0:ROWS, :] = high[:, lanes]
                    beam_ref[2 * n + q, 128 : 128 + ROWS, :] = low[:, lanes]
            return carry

        return tile

    project(((0, 0), (0, 1)), True, False)
    for half in range(2):
        for k in range(2):
            near_copies[half][k].wait_recv()
            far_copies[half][k].start()
        project(((3, half), (1, half)), False, False)
    for c in far_copies[0] + far_copies[1]:
        c.wait_recv()
    project(((2, 0), (2, 1)), False, True)
    pl.when(has_after)(step.wait_send)
    for half in range(2):
        pl.when(has_before)(steps[half].wait_send)
        for c in near_copies[half] + far_copies[half]:
            c.wait_send()
    wide_ref[...] = jnp.zeros_like(wide_ref)

    def square(i, carry):
        part = jnp.concatenate([beam_ref[16 * i + k] for k in range(16)], axis=1)
        wide_ref[...] += lax.dot_general(
            part, part[0:128], (((1,), (1,)), ((), ())), preferred_element_type=F32
        )
        return carry

    lax.fori_loop(0, 2, square, 0)
    cross = wide_ref[128:256, :]
    gram = wide_ref[0:128, :] + cross + cross.T
    for k in range(32):
        mine_ref[k] = gram[4 * k : 4 * k + 4]

    def exchange(stage, moves, all_sent, all_received):
        for source, target, place in moves:
            copy(source, target, place, send, recv, stage).start()
        every = copy(all_sent, all_received, moves[0][2], send, recv, stage)
        every.wait_recv()
        return every

    def added(values):
        while len(values) > 1:
            values = [
                values[i] + values[i + 1] if i + 1 < len(values) else values[i]
                for i in range(0, len(values), 2)
            ]
        return values[0]

    pl.semaphore_wait(ready_sem, 3)
    stages = [None] * 3
    stages[0] = exchange(
        0,
        [(mine_ref.at[peer], got_ref.at[k], place) for k, (peer, place) in enumerate(around)],
        mine_ref.at[0:31],
        got_ref.at[0:31],
    )
    total = added([mine_ref[me]] + [got_ref[k] for k in range(31)])
    sum_ref[...] = total
    stages[1] = exchange(
        1,
        [(sum_ref, got_ref.at[31 + k], place) for k, place in enumerate(along_z)],
        mine_ref.at[0:7],
        got_ref.at[31:38],
    )
    total = added([total] + [got_ref[31 + k] for k in range(7)])
    gram_ref[me] = total
    stages[2] = exchange(
        2,
        [(gram_ref.at[me], gram_ref.at[me], place) for _, place in around],
        mine_ref.at[0:31],
        gram_ref.at[0:31],
    )

    gram = jnp.concatenate([gram_ref[k] for k in range(32)], axis=0)
    basis_ref[...] = jnp.zeros_like(basis_ref)
    basis_ref[0:RANK, 0:FRAMES] = prior_ref[...]
    lane = iota((32, 128), 1)
    odd = (lane >= SIDE).astype(jnp.int32)
    frame = 2 * (lane - SIDE * odd) + odd
    basis = jnp.take_along_axis(basis_ref[...], jnp.minimum(frame, 127), axis=1)
    basis = jnp.where(frame < FRAMES, basis, 0.0)
    basis = sweep(gram, basis)
    basis = sweep(gram, basis)
    overlap = lax.dot_general(
        basis,
        basis,
        (((0,), (0,)), ((), ())),
        precision=lax.Precision.HIGHEST,
        preferred_element_type=F32,
    )
    keep = jnp.where(iota((128, 128), 0) == iota((128, 128), 1), 1.0, 0.0) - overlap
    high = keep.astype(BF16)
    low = (keep - high.astype(F32)).astype(BF16)
    twice = jnp.concatenate([high, high], axis=1)
    for c in range(VOXELS // 256):
        beam = jnp.concatenate([beam_ref[2 * c], beam_ref[2 * c + 1]], axis=1)
        clean = jnp.dot(twice, beam, preferred_element_type=F32)
        clean = clean + jnp.dot(low, beam[0:128], preferred_element_type=F32)
        power = jnp.sum(clean * clean, axis=0, keepdims=True)
        power_ref[2 * c : 2 * c + 1, :] = power[:, 0:128]
        power_ref[2 * c + 1 : 2 * c + 2, :] = power[:, 128:256]
    for stage in stages:
        stage.wait_send()
    pick = (2 * (sub8 & 3) + (lane8 >> 6)) * 16 + (lane8 & 15)
    quarter = (lane8 >> 4) & 3
    for p in range(4):
        rows = None
        for q in range(4):
            one = jnp.broadcast_to(power_ref[8 * q + 2 * p : 8 * q + 2 * p + 1, :], (8, 128))
            two = jnp.broadcast_to(power_ref[8 * q + 2 * p + 1 : 8 * q + 2 * p + 2, :], (8, 128))
            got = jnp.take_along_axis(jnp.where(sub8 < 4, one, two), pick, axis=1)
            rows = got if rows is None else jnp.where(quarter == q, got, rows)
        out_ref[8 * p : 8 * p + 8, :] = rows


def body(echo_data, delays, aperture, offset, depth_slope, lateral_tilt, prior_basis):
    vmem = pl.BlockSpec(memory_space=VMEM)
    dma = pltpu.SemaphoreType.DMA
    squares = pl.pallas_call(
        kernel,
        out_shape=VMEM((VOXELS // 128, 128), F32),
        in_specs=[pl.BlockSpec(memory_space=pl.ANY)] * 7,
        out_specs=vmem,
        scratch_shapes=[
            pltpu.SMEM((2, 128), jnp.int32),
            VMEM((SLABS, 128), jnp.int32),
            VMEM((1, 256), jnp.int32),
            VMEM((1, 128), F32),
            VMEM((1, 128), F32),
            VMEM((1, 128), F32),
            VMEM((RANK, FRAMES), F32),
            VMEM((GROUP, 8, 128 * PAIRS), BF16),
            VMEM((PAIRS, 64, 128), BF16),
            VMEM((HALF + 56, 128), F32),
            VMEM((2, HALF, 128), F32),
            VMEM((2, HALF, 128), BF16),
            VMEM((2, HALF, 128), BF16),
            VMEM((1, 256), jnp.int32),
            VMEM((4, SIZE, 128), BF16),
            VMEM((4, 2, 3, 8, 128), F32),
            VMEM((384, 128), F32),
            VMEM((ROWS, VOXELS), F32),
            VMEM((VOXELS // 128, 256, 128), BF16),
            VMEM((256, 128), F32),
            VMEM((32, 4, 128), F32),
            VMEM((38, 4, 128), F32),
            VMEM((4, 128), F32),
            VMEM((32, 4, 128), F32),
            VMEM((32, 128), F32),
            VMEM((VOXELS // 128, 128), F32),
            pltpu.SemaphoreType.REGULAR,
            dma((9,)),
            dma((3,)),
            dma((3,)),
            dma((8,)),
            dma((8,)),
            dma((3,)),
            dma((3,)),
        ],
        compiler_params=pltpu.CompilerParams(
            collective_id=0, has_side_effects=True, vmem_limit_bytes=62 * 1024 * 1024
        ),
        name="doppler",
    )(
        aperture.T,
        delays.reshape(1, 256),
        offset.reshape(1, 128),
        depth_slope.reshape(1, 128),
        lateral_tilt.reshape(1, 128),
        prior_basis.T,
        echo_data.reshape(GROUP, 8, 128 * PAIRS),
    )
    return squares.reshape(1, VOXELS) / FRAMES


def solution(mesh):
    in_specs = (
        P("chan", "vox", None),
        P("chan", "vox"),
        P(),
        P(None, "vox"),
        P(None, "vox"),
        P(None, "vox"),
        P(),
    )
    out_specs = P("vox", "chan")
    return jax.shard_map(body, mesh=mesh, in_specs=in_specs, out_specs=out_specs, check_vma=False)
```
